32 devices in a mesh: comp: 2 (over x), tile: 16 (over z, y, core).
Axes of the slice: x: 2, y: 2, z: 4, core: 2. Of those that a mesh axis runs over, the one named last changes fastest.
Arguments:
- atm_state: bfloat16 [256, 1024, 256], P(None, ('comp', 'tile')), may hold values from -6 to 6
- atm_sea: int32 [1024, 256], P(('comp', 'tile')), may hold values 0 or 1
- zonal_courant: float32 [256], replicated, may hold values from 0.05 to 0.45
- atm_vertical: bfloat16 [256, 256], replicated, may hold values from -1 to 1
- ocean_state: float32 [160, 512, 128], P(None, ('comp', 'tile')), may hold values from -6 to 6
- ocean_sea: int32 [512, 128], P(('comp', 'tile')), may hold values 0 or 1
- flux_in: float32 [2, 512, 128], P(None, ('comp', 'tile')), may hold values from -6 to 6
- ocean_vertical: float32 [160, 160], replicated, may hold values from -1 to 1
- remap_owner: int32 [2048, 4], P(('comp', 'tile')), may hold values from 0 to 31, all different within a row; in each aligned block of 64 rows (0 to 63, 64 to 127, ...) at most 16 rows name the same one
- remap_block: int32 [2048, 4], P(('comp', 'tile')), may hold values from 0 to 15
- remap_weight: bfloat16 [2048, 4, 128, 128], P(('comp', 'tile')), may hold values from 0 to 0.00390625
Outputs:
- atm_next: bfloat16 [256, 1024, 256], P(None, ('comp', 'tile'))
- ocean_next: float32 [160, 512, 128], P(None, ('comp', 'tile'))
- ocean_flux: float32 [2, 512, 128], P(None, ('comp', 'tile'))
The draws below stay inside these ranges and needn't reach their ends.
Inputs may be any that keep to these rules, and one draw needn't show every extreme that they name: `remap_owner`: in each row 4 different owners; among the 64 rows of one device no owner appears more than 16 times, a bound that some block reaches.
All inputs are finite; a program needn't handle non-finite values. No bound on the sum of `atm_sea` or of `ocean_sea` on one device may be relied on, other than what follows from the above.
Results may differ from the reference program's by a relative error of at most 0.0056.
Values may be sent and summed in bfloat16 or wider, within the bound.
A program may use at most 128 MiB of HBM per device.

```python
import math
import jax
import jax.numpy as jnp
import numpy as np
from jax import lax

LA = 128
LO = 80
AX = 32
AY = 256
BLK = 128
K = 4
OY = 128
NAX = 1024
NOX = 512
ABLK = 64
OBLK = 16
ATM_BLOCKS = 2048
CAP = 16
OWNERS = 32


def draw_atm_vertical(key, part):
    order = 2 * LA
    spread = 0.5 * math.sqrt(3.0 / order)
    noise = jax.random.uniform(key, (order, order), jnp.float32, -1.0, 1.0) * spread
    return (0.7 * jnp.eye(order, dtype=jnp.float32) + noise).astype(jnp.bfloat16)


def draw_ocean_vertical(key, part):
    order = 2 * LO
    spread = 0.5 * math.sqrt(3.0 / order)
    noise = jax.random.uniform(jax.random.fold_in(key, 7), (order, order), jnp.float32, -1.0, 1.0) * spread
    return 0.7 * jnp.eye(order, dtype=jnp.float32) + noise


def touch_ends(drawn, rng, smallest, largest):
    spot = [jax.random.randint(jax.random.fold_in(rng, axis), (), 0, length) for axis, length in enumerate(drawn.shape)]
    longest = drawn.shape.index(max(drawn.shape))
    beside = spot[:longest] + [(spot[longest] + 1) % drawn.shape[longest]] + spot[longest + 1:]
    return drawn.at[tuple(spot)].set(smallest).at[tuple(beside)].set(largest)


def steps_of(rng, extent, cuts, low, high):
    level = 1.0
    for axis_at, parts in cuts:
        heights = jax.random.uniform(jax.random.fold_in(jax.random.fold_in(rng, 6), axis_at), (parts,), jnp.float32, low / len(cuts), high / len(cuts))
        level = level * jnp.repeat(jnp.exp(heights), extent[axis_at] // parts).reshape((-1,) + (1,) * (len(extent) - 1 - axis_at))
    return level


def assign_block(stream_key, own, number, rows, count, top, bound, lean):
    ranking = jax.random.permutation(stream_key, count)
    packed, ordinary = load_shares(count, rows * top, bound, lean, True), load_shares(count, rows * top, bound, lean, False)
    places = jnp.arange(count)

    def named(sizes, turn):
        used = int((sizes > 0).sum())
        fixed = max(1, used // 4)
        passed = fixed + (places - fixed + turn * (used - fixed)) % max(1, count - fixed)
        return jnp.zeros((count,), jnp.int32).at[ranking[jnp.where(places < fixed, places, passed)]].set(jnp.asarray(sizes, jnp.int32))

    sizes = jnp.where(number % 4 == 0, named(packed, number // 4), named(ordinary, number - number // 4 - 1))
    mixed = jax.random.permutation(jax.random.fold_in(own, 3), count)
    source_of, receiver = mixed[0:count // 2 * 2:2], mixed[1:count // 2 * 2:2]
    margin = jnp.minimum(sizes[source_of] - 1, bound - sizes[receiver]) // 2
    margin = jnp.where((source_of == ranking[0]) | (receiver == ranking[0]) | (sizes[receiver] == 0), 0, jnp.maximum(margin, 0))
    passed = jax.random.randint(jax.random.fold_in(own, 4), (count // 2,), 0, 1 << 20) % (margin + 1)
    sizes = sizes.at[source_of].add(-passed).at[receiver].add(passed)
    items = jnp.searchsorted(jnp.cumsum(sizes), jnp.arange(rows * top), side="right").astype(jnp.int32)
    table = items.reshape(top, rows).T
    table = table[jax.random.permutation(jax.random.fold_in(own, 1), rows)]
    turn = jax.random.randint(jax.random.fold_in(own, 2), (rows, 1), 0, top)
    return jnp.take_along_axis(table, (jnp.arange(top)[None, :] + turn) % top, axis=1)


def load_shares(count, total, reach, slope, full):
    weights = [(1 << 20) // math.isqrt(grade ** slope) + 1 for grade in range(1, count + 1)]
    largest = reach if full else min(reach, max(-(-total // count), total * weights[0] // sum(weights)))
    least = 1 if total - largest >= count - 1 else 0
    holding, surplus = [largest] + [least] * (count - 1), total - largest - least * (count - 1)
    while surplus > 0:
        movable = [i for i in range(1, count) if holding[i] < largest] or [i for i in range(1, count) if holding[i] < reach]
        mass, left = sum([weights[i] for i in movable]), surplus
        for i in movable:
            more = min(reach - holding[i], max(1, left * weights[i] // mass), surplus)
            holding[i] = holding[i] + more
            surplus = surplus - more
    return np.array(holding)


def scatter_about(own_key, shape, deviation, bound, cuts=(), held_as=jnp.bfloat16):
    factor_of = steps_of(own_key, shape, cuts, -0.22, 0.18) if cuts else 1.0
    drawn = jax.random.normal(own_key, shape, jnp.float32) * deviation * factor_of
    return jnp.minimum(jnp.maximum(drawn, -bound), bound).astype(held_as)


def setup_inputs(seed: int = 0) -> dict:
    streams_of = jax.random.split(jax.random.key(seed), 12)
    atm_state = scatter_about(streams_of[0], (2 * LA, NAX, AY), 1.0, 6.0, ((1, 32),))
    atm_sea = touch_ends((jax.random.randint(streams_of[1], (NAX, AY), 0, 3) < 2).astype(jnp.int32), jax.random.fold_in(streams_of[1], 1), 0, 1)
    zonal_courant = jnp.clip(jnp.exp(jax.random.uniform(streams_of[2], (2 * LA,), jnp.float32, math.log(0.05), math.log(0.45))), 0.05, 0.45)
    atm_vertical = draw_atm_vertical(jax.random.fold_in(streams_of[11], 71), 0)
    ocean_state = scatter_about(streams_of[4], (2 * LO, NOX, OY), 1.0, 6.0, ((1, 32),), jnp.float32)
    ocean_sea = touch_ends((jax.random.randint(streams_of[5], (NOX, OY), 0, 4) < 3).astype(jnp.int32), jax.random.fold_in(streams_of[5], 1), 0, 1)
    flux_in = scatter_about(streams_of[6], (2, NOX, OY), 1.0, 6.0, ((1, 32),), jnp.float32)
    ocean_vertical = draw_ocean_vertical(jax.random.fold_in(streams_of[11], 71), 0)
    remap_owner_keys = jax.random.split(jax.random.fold_in(streams_of[8], 1), ATM_BLOCKS // ABLK)
    remap_owner_turns = jax.random.permutation(jax.random.fold_in(streams_of[8], 3), ATM_BLOCKS // ABLK)
    remap_owner = jax.vmap(lambda own, number: assign_block(jax.random.fold_in(streams_of[8], 2), own, number, ABLK, OWNERS, K, CAP, 1))(remap_owner_keys, remap_owner_turns).reshape((ATM_BLOCKS, K))
    remap_block = touch_ends(jax.random.randint(streams_of[9], (ATM_BLOCKS, K), 0, OBLK), jax.random.fold_in(streams_of[9], 1), 0, OBLK - 1).astype(jnp.int32)
    remap_weight = jnp.clip(0.00390625 * jax.random.uniform(streams_of[10], (ATM_BLOCKS, K, BLK, BLK), jnp.float32) ** steps_of(streams_of[10], (ATM_BLOCKS, K, BLK, BLK), ((0, 32),), -0.2, 0.2), 0.0, 0.00390625).astype(jnp.bfloat16)
    return {"atm_state": atm_state, "atm_sea": atm_sea, "zonal_courant": zonal_courant, "atm_vertical": atm_vertical, "ocean_state": ocean_state, "ocean_sea": ocean_sea, "flux_in": flux_in, "ocean_vertical": ocean_vertical, "remap_owner": remap_owner, "remap_block": remap_block, "remap_weight": remap_weight}


ATM_DIFFUSION = 0.1
OCEAN_DIFFUSION = 0.15
EXCHANGE_RATE = 0.3
FLUX_GAIN = 0.5


def lateral_sum(center):
    north = jnp.concatenate([center[:, :, 1:], center[:, :, -1:]], axis=2)
    south = jnp.concatenate([center[:, :, :1], center[:, :, :-1]], axis=2)
    return north + south


def atmos_advance(padded, sea_temp, sea_frac, courant, vertical):
    height = padded.shape[0]
    levels = height // 2
    center = padded[:, 1:-1].astype(jnp.float32)
    west_side = padded[:, :-2].astype(jnp.float32)
    east_side = padded[:, 2:].astype(jnp.float32)
    tendency = east_side + west_side + lateral_sum(center) - 4.0 * center
    updated = center - courant[:, None, None] * (center - west_side) + ATM_DIFFUSION * tendency
    heat_flux = EXCHANGE_RATE * sea_frac * (sea_temp - updated[levels - 1])
    moist_flux = EXCHANGE_RATE * sea_frac * (0.5 * sea_temp - updated[2 * levels - 1])
    rows = lax.broadcasted_iota(jnp.int32, (height, 1, 1), 0)
    added = jnp.where(rows == levels - 1, heat_flux[None], jnp.where(rows == 2 * levels - 1, moist_flux[None], jnp.zeros_like(heat_flux)[None]))
    forced = (updated + added).astype(jnp.bfloat16)
    mixed = jnp.dot(vertical, forced.reshape(height, -1), preferred_element_type=jnp.float32)
    return mixed.reshape(forced.shape).astype(jnp.bfloat16), heat_flux, moist_flux


def ocean_advance(padded, sea_frac, flux_old, vertical):
    height = padded.shape[0]
    levels = height // 2
    center = padded[:, 1:-1]
    tendency = padded[:, 2:] + padded[:, :-2] + lateral_sum(center) - 4.0 * center
    rows = lax.broadcasted_iota(jnp.int32, (height, 1, 1), 0)
    heat_in = FLUX_GAIN * sea_frac * flux_old[0]
    fresh_in = FLUX_GAIN * sea_frac * flux_old[1]
    added = jnp.where(rows == 0, heat_in[None], jnp.where(rows == levels, fresh_in[None], jnp.zeros_like(heat_in)[None]))
    updated = (center + OCEAN_DIFFUSION * tendency) * sea_frac + added
    mixed = jnp.dot(vertical, updated.reshape(height, -1), precision=lax.Precision.HIGHEST, preferred_element_type=jnp.float32)
    return mixed.reshape(updated.shape)


def wrap_columns(field):
    return jnp.concatenate([field[:, -1:], field, field[:, :1]], axis=1)


def atmos_global(state, sea_temp, sea_atm, courant, vertical):
    groups = state.shape[1] // AX
    wrapped = wrap_columns(state)

    def advance_group(index):
        start = (index * AX).astype(jnp.int32)
        padded = lax.dynamic_slice_in_dim(wrapped, start, AX + 2, 1)
        temps = lax.dynamic_slice_in_dim(sea_temp, start, AX, 0)
        fracs = lax.dynamic_slice_in_dim(sea_atm, start, AX, 0)
        new_part, heat_part, moist_part = atmos_advance(padded, temps, fracs, courant, vertical)
        return new_part, jnp.stack([heat_part, moist_part])

    new_parts, flux_parts = lax.map(advance_group, jnp.arange(groups, dtype=jnp.int32))
    new_state = jnp.moveaxis(new_parts, 0, 1).reshape(state.shape)
    fluxes = jnp.moveaxis(flux_parts, 0, 1).reshape((2,) + sea_atm.shape)
    return new_state, fluxes


def reference(atm_state, atm_sea, zonal_courant, atm_vertical, ocean_state, ocean_sea, flux_in, ocean_vertical, remap_owner, remap_block, remap_weight):
    sea_atm = atm_sea.astype(jnp.float32)
    sea_ocean = ocean_sea.astype(jnp.float32)
    ocean_blocks = ocean_state[0].reshape(-1, BLK).astype(jnp.bfloat16)
    targets = (remap_owner * OBLK + remap_block).astype(jnp.int32)
    groups = ATM_BLOCKS // ABLK
    weights = remap_weight.reshape(groups, ABLK, K, BLK, BLK)
    fetched = ocean_blocks[targets].reshape(groups, ABLK, K, BLK)

    def pull(pair):
        weight_part, fetched_part = pair
        return jnp.einsum("jkao,jko->ja", weight_part.astype(jnp.float32), fetched_part.astype(jnp.float32), precision=lax.Precision.HIGHEST)

    sea_temp = lax.map(pull, (weights, fetched)).reshape(atm_sea.shape)
    state = atm_state
    flux_sum = jnp.zeros((2,) + atm_sea.shape, jnp.float32)
    for which_step in range(2):
        state, fluxes = atmos_global(state, sea_temp, sea_atm, zonal_courant, atm_vertical)
        flux_sum = flux_sum + 0.5 * fluxes
    flux_blocks = flux_sum.astype(jnp.bfloat16).reshape(2, groups, ABLK, BLK)

    def push(pair):
        weight_part, flux_part = pair
        return jnp.einsum("jkao,vja->jkvo", weight_part.astype(jnp.float32), flux_part.astype(jnp.float32), precision=lax.Precision.HIGHEST)

    shares = lax.map(push, (weights, jnp.moveaxis(flux_blocks, 1, 0)))
    summed = jax.ops.segment_sum(shares.reshape(-1, 2, BLK), targets.reshape(-1), num_segments=ocean_blocks.shape[0])
    ocean_flux = jnp.moveaxis(summed, 1, 0).reshape((2,) + ocean_sea.shape) * sea_ocean
    new_ocean = ocean_advance(wrap_columns(ocean_state), sea_ocean, flux_in, ocean_vertical)
    return state, new_ocean, ocean_flux
```

```python
import functools

import jax
import jax.numpy as jnp
from jax import lax
from jax.experimental import pallas as pl
from jax.experimental.pallas import tpu as pltpu
from jax.sharding import PartitionSpec as P

ATM_DIFFUSION = 0.1
OCEAN_DIFFUSION = 0.15
EXCHANGE_RATE = 0.3
FLUX_GAIN = 0.5
MESH = pl.DeviceIdType.MESH
AXES = ("comp", "tile")
F32 = jnp.float32
BF16 = jnp.bfloat16
G = 16
VMEM = pl.BlockSpec(memory_space=pltpu.VMEM)
LIMIT = 60 * 1024 * 1024


def iota(shape, dim):
    return lax.broadcasted_iota(jnp.int32, shape, dim)


def swap_matrix():
    a = iota((G * G, G * G), 0)
    b = iota((G * G, G * G), 1)
    return ((a // G == b % G) & (a % G == b // G)).astype(F32).astype(BF16)


def lateral_matrix(n):
    a = iota((n, n), 0)
    b = iota((n, n), 1)
    north = a == jnp.minimum(b + 1, n - 1)
    south = a == jnp.maximum(b - 1, 0)
    return (north.astype(F32) + south.astype(F32)).astype(BF16)


def dot(a, b):
    return jnp.dot(a, b, preferred_element_type=F32)


def dot_nt(a, b):
    return lax.dot_general(a, b, (((1,), (1,)), ((), ())), preferred_element_type=F32)


def dot_tn(a, b):
    return lax.dot_general(a, b, (((0,), (0,)), ((), ())), preferred_element_type=F32)


def prepare_kernel(st_ref, oc_ref, xs_ref, sst_ref, edge_ref):
    swap = swap_matrix()
    columns = st_ref.shape[2]

    @pl.loop(0, st_ref.shape[0] // G)
    def _(rb):
        r0 = pl.multiple_of(rb * G, G)
        block = st_ref[pl.ds(r0, G)].reshape(G * G, columns)
        moved = dot(swap, block).astype(BF16).reshape(G, G, columns)
        xs_ref[:, pl.ds(r0, G), :] = moved

    @pl.when(pl.program_id(0) == 0)
    def _():
        rows, width, oy = oc_ref.shape
        sst_ref[...] = oc_ref[0].astype(BF16)
        edge_ref[0] = oc_ref[:, 0, :]
        edge_ref[1] = oc_ref[:, width - 1, :]


def prepare(state, ocean):
    rows, width, cols = state.shape
    orows, ow, oy = ocean.shape
    return pl.pallas_call(
        prepare_kernel,
        grid=(width // G,),
        in_specs=[
            pl.BlockSpec((rows, G, cols), lambda g: (0, g, 0)),
            pl.BlockSpec((orows, ow, oy), lambda g: (0, 0, 0)),
        ],
        out_specs=[
            pl.BlockSpec((G, rows, cols), lambda g: (g, 0, 0)),
            pl.BlockSpec((ow, oy), lambda g: (0, 0)),
            pl.BlockSpec((2, orows, oy), lambda g: (0, 0, 0)),
        ],
        out_shape=[
            jax.ShapeDtypeStruct((width, rows, cols), BF16),
            jax.ShapeDtypeStruct((ow, oy), BF16),
            jax.ShapeDtypeStruct((2, orows, oy), F32),
        ],
        compiler_params=pltpu.CompilerParams(vmem_limit_bytes=LIMIT),
        name="prepare",
    )(state, ocean)


def place(index, tiles):
    return (index // tiles, index % tiles)


def my_index(tiles):
    return lax.axis_index("comp") * tiles + lax.axis_index("tile")


def greet_all(n, tiles, me):
    barrier = pltpu.get_barrier_semaphore()

    def signal(d, carry):
        pl.semaphore_signal(barrier, inc=1, device_id=place((me + d) % n, tiles), device_id_type=MESH)
        return carry

    lax.fori_loop(1, n, signal, 0)
    pl.semaphore_wait(barrier, n - 1)


def first_exchange_kernel(n, tiles, sst_ref, edge_ref, xs_ref, all_ref, halo_ref, ohalo_ref, ssem, rsem, hs, hr, local):
    me = my_index(tiles)
    greet_all(n, tiles, me)
    east = place((me + 1) % n, tiles)
    west = place((me + n - 1) % n, tiles)
    width = xs_ref.shape[0]

    def copy(d):
        return pltpu.make_async_remote_copy(
            src_ref=sst_ref, dst_ref=all_ref.at[me], send_sem=ssem.at[d], recv_sem=rsem.at[d],
            device_id=place((me + d) % n, tiles), device_id_type=MESH)

    def start(d, carry):
        copy(d).start()
        return carry

    lax.fori_loop(1, n, start, 0)
    moves = [
        (xs_ref.at[width - 1], halo_ref.at[0], east),
        (xs_ref.at[0], halo_ref.at[1], west),
        (edge_ref.at[1], ohalo_ref.at[0], east),
        (edge_ref.at[0], ohalo_ref.at[1], west),
    ]
    copies = [
        pltpu.make_async_remote_copy(
            src_ref=s, dst_ref=d, send_sem=hs.at[i], recv_sem=hr.at[i], device_id=to, device_id_type=MESH)
        for i, (s, d, to) in enumerate(moves)
    ]
    for c in copies:
        c.start()
    own = pltpu.make_async_copy(sst_ref, all_ref.at[me], local)
    own.start()
    own.wait()

    def finish(d, carry):
        copy(d).wait()
        return carry

    lax.fori_loop(1, n, finish, 0)
    for c in copies:
        c.wait()


def first_exchange(n, tiles, sst, edge, xs):
    width, rows, cols = xs.shape
    dma = pltpu.SemaphoreType.DMA
    return pl.pallas_call(
        functools.partial(first_exchange_kernel, n, tiles),
        in_specs=[VMEM, VMEM, pl.BlockSpec(memory_space=pl.ANY)],
        out_specs=[VMEM, VMEM, VMEM],
        out_shape=[
            jax.ShapeDtypeStruct((n,) + sst.shape, BF16),
            jax.ShapeDtypeStruct((2, rows, cols), BF16),
            jax.ShapeDtypeStruct(edge.shape, F32),
        ],
        scratch_shapes=[dma((n,)), dma((n,)), dma((4,)), dma((4,)), dma],
        compiler_params=pltpu.CompilerParams(collective_id=0, has_side_effects=True, vmem_limit_bytes=16 * 1024 * 1024),
        name="first_exchange",
    )(sst, edge, xs)


def halo_exchange_kernel(n, tiles, xs_ref, halo_ref, hs, hr):
    me = my_index(tiles)
    east = place((me + 1) % n, tiles)
    west = place((me + n - 1) % n, tiles)
    barrier = pltpu.get_barrier_semaphore()
    for to in (east, west):
        pl.semaphore_signal(barrier, inc=1, device_id=to, device_id_type=MESH)
    pl.semaphore_wait(barrier, 2)
    width = xs_ref.shape[0]
    copies = [
        pltpu.make_async_remote_copy(
            src_ref=xs_ref.at[s], dst_ref=halo_ref.at[i], send_sem=hs.at[i], recv_sem=hr.at[i],
            device_id=to, device_id_type=MESH)
        for i, (s, to) in enumerate(((width - 1, east), (0, west)))
    ]
    for c in copies:
        c.start()
    for c in copies:
        c.wait()


def halo_exchange(n, tiles, xs):
    width, rows, cols = xs.shape
    dma = pltpu.SemaphoreType.DMA
    return pl.pallas_call(
        functools.partial(halo_exchange_kernel, n, tiles),
        in_specs=[pl.BlockSpec(memory_space=pl.ANY)],
        out_specs=VMEM,
        out_shape=jax.ShapeDtypeStruct((2, rows, cols), BF16),
        scratch_shapes=[dma((2,)), dma((2,))],
        compiler_params=pltpu.CompilerParams(collective_id=1, has_side_effects=True, vmem_limit_bytes=16 * 1024 * 1024),
        name="halo_exchange",
    )(xs)


def flux_exchange_kernel(n, tiles, acc_ref, sea_ref, out_ref, land, ssem, rsem):
    me = my_index(tiles)
    greet_all(n, tiles, me)

    def copy(d):
        to = (me + d) % n
        return pltpu.make_async_remote_copy(
            src_ref=acc_ref.at[to], dst_ref=land.at[d], send_sem=ssem.at[d], recv_sem=rsem.at[d],
            device_id=place(to, tiles), device_id_type=MESH)

    def start(d, carry):
        copy(d).start()
        return carry

    lax.fori_loop(1, n, start, 0)

    def finish(d, total):
        copy(d).wait()
        return total + land[d].astype(F32)

    total = lax.fori_loop(1, n, finish, acc_ref[me].astype(F32))
    sea = sea_ref[...].astype(F32)
    block = sea.shape[1]
    out_ref[0] = total[:, :block] * sea
    out_ref[1] = total[:, block:] * sea


def flux_exchange(n, tiles, acc, sea):
    dma = pltpu.SemaphoreType.DMA
    return pl.pallas_call(
        functools.partial(flux_exchange_kernel, n, tiles),
        in_specs=[VMEM, VMEM],
        out_specs=VMEM,
        out_shape=jax.ShapeDtypeStruct((2,) + sea.shape, F32),
        scratch_shapes=[pltpu.VMEM(acc.shape, BF16), dma((n,)), dma((n,))],
        compiler_params=pltpu.CompilerParams(collective_id=2, has_side_effects=True, vmem_limit_bytes=16 * 1024 * 1024),
        name="flux_exchange",
    )(acc, sea)


def one_hot(owner_ref, block_ref, k, count, per):
    target = owner_ref[k : k + 1, :] * per + block_ref[k : k + 1, :]
    return (iota((count, target.shape[1]), 0) == target).astype(F32).astype(BF16)


def slab_update(xs_ref, halo_ref, x, first, last, cr, lateral):
    width = xs_ref.shape[0]
    center = xs_ref[x]
    west = xs_ref[jnp.maximum(x - 1, 0)]
    east = xs_ref[jnp.minimum(x + 1, width - 1)]
    if first:
        west = jnp.where(x == 0, halo_ref[0], west)
    if last:
        east = jnp.where(x == width - 1, halo_ref[1], east)
    sides = dot(center, lateral) + east.astype(F32)
    return (
        (1.0 - 4.0 * ATM_DIFFUSION - cr) * center.astype(F32)
        + (cr + ATM_DIFFUSION) * west.astype(F32)
        + ATM_DIFFUSION * sides
    )


def force(updated, f_ref, heat, moist):
    rows = updated.shape[0]
    half = rows // 2
    f_ref[...] = updated.astype(BF16)
    last = iota((G, 1), 0) == G - 1
    for end, added in ((half, heat), (rows, moist)):
        part = updated[end - G : end]
        f_ref[end - G : end, :] = jnp.where(last, part + added, part).astype(BF16)


def step_one_kernel(xs_ref, halo_ref, all_ref, owner_ref, block_ref, w_ref, sea_ref, cr_ref, v_ref,
                    new_ref, temp_ref, heat_ref, moist_ref, r0_ref, r1_ref, fetched, forced):
    g = pl.program_id(0)
    xg = new_ref.shape[0]
    jg, kk, block, _ = w_ref.shape
    count = all_ref.shape[0] * all_ref.shape[1]

    @pl.when(g == 0)
    def _():
        table = all_ref[...].reshape(count, block)
        for k in range(kk):
            hot = one_hot(owner_ref, block_ref, k, count, all_ref.shape[1])
            fetched[k] = dot_tn(hot, table).astype(BF16)

    rows = xs_ref.shape[1]
    half = rows // 2
    lateral = lateral_matrix(xs_ref.shape[2])
    vertical = v_ref[...]
    cr = cr_ref[...]
    j0 = pl.multiple_of(g * jg, jg)
    sources = [fetched[k, pl.ds(j0, jg), :] for k in range(kk)]
    per = jg // xg
    for i in range(xg):
        temps = []
        for j in range(per * i, per * i + per):
            total = dot_nt(sources[0], w_ref[j, 0])
            for k in range(1, kk):
                total = total + dot_nt(sources[k], w_ref[j, k])
            temps.append(total[j : j + 1])
        temp = jnp.concatenate(temps, axis=1)
        updated = slab_update(xs_ref, halo_ref, g * xg + i, i == 0, i == xg - 1, cr, lateral)
        sea = EXCHANGE_RATE * sea_ref[i : i + 1, :].astype(F32)
        heat = sea * (temp - updated[half - 1 : half])
        moist = sea * (0.5 * temp - updated[rows - 1 : rows])
        slot = forced.at[i % 2]
        force(updated, slot, heat, moist)
        mixed = dot(vertical, slot[...]).astype(BF16)
        new_ref[i] = mixed
        temp_ref[i : i + 1, :] = temp
        heat_ref[i : i + 1, :] = heat
        moist_ref[i : i + 1, :] = moist
        r0_ref[i : i + 1, :] = mixed[half - G : half].astype(F32)[G - 1 : G]
        r1_ref[i : i + 1, :] = mixed[rows - G : rows].astype(F32)[G - 1 : G]


def whole(shape):
    return pl.BlockSpec(shape, lambda g: (0,) * len(shape))


def step_one(xs, halo, all_sst, owner, blocks, weight, sea, cr, vertical):
    width, rows, cols = xs.shape
    jb, kk, block, _ = weight.shape
    xg = 8
    steps = width // xg
    jg = jb // steps
    row = pl.BlockSpec((xg, cols), lambda g: (g, 0))
    rowshape = jax.ShapeDtypeStruct((width, cols), F32)
    return pl.pallas_call(
        step_one_kernel,
        grid=(steps,),
        in_specs=[
            whole(xs.shape), whole(halo.shape), whole(all_sst.shape), whole(owner.shape), whole(blocks.shape),
            pl.BlockSpec((jg, kk, block, block), lambda g: (g, 0, 0, 0)),
            row, whole(cr.shape), whole(vertical.shape),
        ],
        out_specs=[pl.BlockSpec((xg, rows, cols), lambda g: (g, 0, 0))] + [row] * 5,
        out_shape=[jax.ShapeDtypeStruct(xs.shape, BF16)] + [rowshape] * 5,
        scratch_shapes=[pltpu.VMEM((kk, jb, block), BF16), pltpu.VMEM((2, rows, cols), BF16)],
        compiler_params=pltpu.CompilerParams(vmem_limit_bytes=LIMIT),
        name="step_one",
    )(xs, halo, all_sst, owner, blocks, weight, sea, cr, vertical)


def push_kernel(r0_ref, r1_ref, halo_ref, cr_ref, sea_ref, temp_ref, heat_ref, moist_ref, owner_ref, block_ref, w_ref,
                heat2_ref, moist2_ref, acc_ref, mean, shares):
    g = pl.program_id(0)
    width, cols = r0_ref.shape
    jg, kk, block, _ = w_ref.shape
    rows = halo_ref.shape[1]
    per_owner = acc_ref.shape[1]

    @pl.when(g == 0)
    def _():
        lateral = lateral_matrix(cols)
        sea = EXCHANGE_RATE * sea_ref[...].astype(F32)
        temp = temp_ref[...]
        for v, (ref, end, gain, old, out) in enumerate((
            (r0_ref, rows // 2, 1.0, heat_ref, heat2_ref),
            (r1_ref, rows, 0.5, moist_ref, moist2_ref),
        )):
            center = ref[...]
            hw = halo_ref[0, end - G : end, :].astype(F32)[G - 1 : G]
            he = halo_ref[1, end - G : end, :].astype(F32)[G - 1 : G]
            west = jnp.concatenate([hw, center[:-1]], axis=0)
            east = jnp.concatenate([center[1:], he], axis=0)
            cr = cr_ref[end - 1 : end, :]
            updated = (
                (1.0 - 4.0 * ATM_DIFFUSION - cr) * center
                + (cr + ATM_DIFFUSION) * west
                + ATM_DIFFUSION * (dot(center.astype(BF16), lateral) + east)
            )
            flux = sea * (gain * temp - updated)
            out[...] = flux
            mean[v] = (0.5 * old[...] + 0.5 * flux).astype(BF16).astype(F32)

    xg = width * jg // owner_ref.shape[1]
    per = jg // xg
    x0 = pl.multiple_of(g * xg, xg)
    lefts = [
        jnp.concatenate([mean[v, pl.ds(x0, xg), h * block : (h + 1) * block] for v in range(2)], axis=0).astype(BF16)
        for h in range(per)
    ]
    j0 = pl.multiple_of(g * jg, jg)
    for k in range(kk):
        rows_of = []
        for j in range(jg):
            i = j // per
            share = dot(lefts[j % per], w_ref[j, k])
            rows_of.append(jnp.concatenate([share[i : i + 1], share[xg + i : xg + i + 1]], axis=1))
        shares[k, pl.ds(j0, jg), :] = jnp.concatenate(rows_of, axis=0)

    @pl.when(g == pl.num_programs(0) - 1)
    def _():
        count = acc_ref.shape[0] * per_owner
        total = jnp.zeros((count, 2 * block), F32)
        for k in range(kk):
            hot = one_hot(owner_ref, block_ref, k, count, per_owner)
            share = shares[k]
            high = share.astype(BF16)
            low = (share - high.astype(F32)).astype(BF16)
            total = total + dot(hot, high) + dot(hot, low)
        acc_ref[...] = total.astype(BF16).reshape(acc_ref.shape)


def push(n, per_owner, r0, r1, halo, cr, sea, temp, heat, moist, owner, blocks, weight):
    width, cols = r0.shape
    jb, kk, block, _ = weight.shape
    steps = width // 8
    jg = jb // steps
    return pl.pallas_call(
        push_kernel,
        grid=(steps,),
        in_specs=[whole(a.shape) for a in (r0, r1, halo, cr, sea, temp, heat, moist, owner, blocks)]
        + [pl.BlockSpec((jg, kk, block, block), lambda g: (g, 0, 0, 0))],
        out_specs=[whole(r0.shape), whole(r0.shape), whole((n, per_owner, 2 * block))],
        out_shape=[
            jax.ShapeDtypeStruct(r0.shape, F32),
            jax.ShapeDtypeStruct(r0.shape, F32),
            jax.ShapeDtypeStruct((n, per_owner, 2 * block), BF16),
        ],
        scratch_shapes=[pltpu.VMEM((2, width, cols), F32), pltpu.VMEM((kk, jb, 2 * block), F32)],
        compiler_params=pltpu.CompilerParams(vmem_limit_bytes=LIMIT),
        name="push",
    )(r0, r1, halo, cr, sea, temp, heat, moist, owner, blocks, weight)


def step_two_kernel(xs_ref, halo_ref, heat_ref, moist_ref, cr_ref, v_ref, out_ref, forced, new):
    g = pl.program_id(0)
    cols = xs_ref.shape[2]
    lateral = lateral_matrix(cols)
    swap = swap_matrix()
    vertical = v_ref[...]
    cr = cr_ref[...]
    for i in range(G):
        updated = slab_update(xs_ref, halo_ref, g * G + i, i == 0, i == G - 1, cr, lateral)
        slot = forced.at[i % 2]
        force(updated, slot, heat_ref[i : i + 1, :], moist_ref[i : i + 1, :])
        new[i] = dot(vertical, slot[...]).astype(BF16)

    @pl.loop(0, out_ref.shape[0] // G)
    def _(rb):
        r0 = pl.multiple_of(rb * G, G)
        block = new[:, pl.ds(r0, G), :].reshape(G * G, cols)
        out_ref[pl.ds(r0, G)] = dot(swap, block).astype(BF16).reshape(G, G, cols)


def step_two(xs, halo, heat, moist, cr, vertical):
    width, rows, cols = xs.shape
    row = pl.BlockSpec((G, cols), lambda g: (g, 0))
    return pl.pallas_call(
        step_two_kernel,
        grid=(width // G,),
        in_specs=[whole(xs.shape), whole(halo.shape), row, row, whole(cr.shape), whole(vertical.shape)],
        out_specs=pl.BlockSpec((rows, G, cols), lambda g: (0, g, 0)),
        out_shape=jax.ShapeDtypeStruct((rows, width, cols), BF16),
        scratch_shapes=[pltpu.VMEM((2, rows, cols), BF16), pltpu.VMEM((G, rows, cols), BF16)],
        compiler_params=pltpu.CompilerParams(vmem_limit_bytes=LIMIT),
        name="step_two",
    )(xs, halo, heat, moist, cr, vertical)


def ocean_kernel(oc_ref, halo_ref, sea_ref, flux_ref, v_ref, out_ref):
    rows, width, cols = oc_ref.shape
    half = rows // 2
    vertical = v_ref[...]
    vhigh = vertical.astype(BF16)
    vlow = (vertical - vhigh.astype(F32)).astype(BF16)
    lane = iota((1, cols), 1)
    row = iota((rows, 1), 0)
    slabs = [halo_ref[0]] + [oc_ref[:, x, :] for x in range(width)] + [halo_ref[1]]
    for x in range(width):
        west, center, east = slabs[x : x + 3]
        north = jnp.where(lane == cols - 1, center, pltpu.roll(center, cols - 1, 1))
        south = jnp.where(lane == 0, center, pltpu.roll(center, 1, 1))
        tendency = east + west + (north + south) - 4.0 * center
        sea = sea_ref[x : x + 1, :].astype(F32)
        heat = FLUX_GAIN * sea * flux_ref[0, x : x + 1, :]
        fresh = FLUX_GAIN * sea * flux_ref[1, x : x + 1, :]
        updated = (center + OCEAN_DIFFUSION * tendency) * sea
        updated = updated + jnp.where(row == 0, heat, jnp.where(row == half, fresh, 0.0))
        high = updated.astype(BF16)
        low = (updated - high.astype(F32)).astype(BF16)
        mixed = dot(vhigh, high) + (dot(vhigh, low) + dot(vlow, high))
        out_ref[:, x, :] = mixed


def ocean_step(ocean, halo, sea, flux, vertical):
    return pl.pallas_call(
        ocean_kernel,
        in_specs=[VMEM] * 5,
        out_specs=VMEM,
        out_shape=jax.ShapeDtypeStruct(ocean.shape, F32),
        compiler_params=pltpu.CompilerParams(vmem_limit_bytes=LIMIT),
        name="ocean_step",
    )(ocean, halo, sea, flux, vertical)


def per_device(n, tiles, atm_state, atm_sea, zonal_courant, atm_vertical, ocean_state, ocean_sea, flux_in,
               ocean_vertical, remap_owner, remap_block, remap_weight):
    owner = remap_owner.T
    blocks = remap_block.T
    cr = zonal_courant.reshape(-1, 1)
    xs, sst, edge = prepare(atm_state, ocean_state)
    all_sst, halo, ohalo = first_exchange(n, tiles, sst, edge, xs)
    new, temp, heat, moist, r0, r1 = step_one(
        xs, halo, all_sst, owner, blocks, remap_weight, atm_sea, cr, atm_vertical)
    halo2 = halo_exchange(n, tiles, new)
    heat2, moist2, acc = push(
        n, sst.shape[0], r0, r1, halo2, cr, atm_sea, temp, heat, moist, owner, blocks, remap_weight)
    ocean_flux = flux_exchange(n, tiles, acc, ocean_sea)
    atm_next = step_two(new, halo2, heat2, moist2, cr, atm_vertical)
    ocean_next = ocean_step(ocean_state, ohalo, ocean_sea, flux_in, ocean_vertical)
    return atm_next, ocean_next, ocean_flux


def solution(mesh):
    tiles = mesh.shape["tile"]
    n = mesh.shape["comp"] * tiles
    return jax.shard_map(
        functools.partial(per_device, n, tiles),
        mesh=mesh,
        in_specs=(
            P(None, AXES, None), P(AXES, None), P(), P(), P(None, AXES, None), P(AXES, None),
            P(None, AXES, None), P(), P(AXES, None), P(AXES, None), P(AXES, None, None, None),
        ),
        out_specs=(P(None, AXES, None), P(None, AXES, None), P(None, AXES, None)),
        check_vma=False,
    )
```

```python
import functools

import jax
import jax.numpy as jnp
from jax import lax
from jax.experimental import pallas as pl
from jax.experimental.pallas import tpu as pltpu
from jax.sharding import PartitionSpec as P

ATM_DIFFUSION = 0.1
OCEAN_DIFFUSION = 0.15
EXCHANGE_RATE = 0.3
FLUX_GAIN = 0.5
MESH = pl.DeviceIdType.MESH
AXES = ("comp", "tile")
F32 = jnp.float32
BF16 = jnp.bfloat16
G = 16
HBM = pl.BlockSpec(memory_space=pltpu.HBM)
LIMIT = 60 * 1024 * 1024


def iota(shape, dim):
    return lax.broadcasted_iota(jnp.int32, shape, dim)


def swap_matrix():
    a = iota((G * G, G * G), 0)
    b = iota((G * G, G * G), 1)
    return ((a // G == b % G) & (a % G == b // G)).astype(F32).astype(BF16)


def lateral_matrix(n):
    a = iota((n, n), 0)
    b = iota((n, n), 1)
    north = a == jnp.minimum(b + 1, n - 1)
    south = a == jnp.maximum(b - 1, 0)
    return (north.astype(F32) + south.astype(F32)).astype(BF16)


def dot(a, b):
    return jnp.dot(a, b, preferred_element_type=F32)


def dot_nt(a, b):
    return lax.dot_general(a, b, (((1,), (1,)), ((), ())), preferred_element_type=F32)


def dot_tn(a, b):
    return lax.dot_general(a, b, (((0,), (0,)), ((), ())), preferred_element_type=F32)


def edges_kernel(lo_ref, hi_ref, oc_ref, xe_ref, sst_ref, edge_ref):
    width = oc_ref.shape[1]
    part = hi_ref.shape[1]
    sst_ref[...] = oc_ref[0].astype(BF16)
    edge_ref[0] = oc_ref[:, 0, :]
    edge_ref[1] = oc_ref[:, width - 1, :]
    swap = swap_matrix()
    picks = (swap[:G], swap[G * G - G :])
    cols = lo_ref.shape[2]
    for rb in range(lo_ref.shape[0] // G):
        for side, ref in enumerate((lo_ref, hi_ref)):
            block = ref[rb * G : (rb + 1) * G].reshape(G * part, cols)
            xe_ref[side, rb * G : (rb + 1) * G, :] = dot(picks[side], block).astype(BF16)


def edges(state, ocean):
    rows, width, cols = state.shape
    orows, ow, oy = ocean.shape
    last = width // G - 1
    return pl.pallas_call(
        edges_kernel,
        grid=(1,),
        in_specs=[
            pl.BlockSpec((rows, G, cols), lambda g: (0, 0, 0)),
            pl.BlockSpec((rows, G, cols), lambda g: (0, last, 0)),
            pl.BlockSpec((orows, ow, oy), lambda g: (0, 0, 0)),
        ],
        out_specs=[
            pl.BlockSpec((2, rows, cols), lambda g: (0, 0, 0)),
            pl.BlockSpec((ow, oy), lambda g: (0, 0)),
            pl.BlockSpec((2, orows, oy), lambda g: (0, 0, 0)),
        ],
        out_shape=[
            jax.ShapeDtypeStruct((2, rows, cols), BF16),
            jax.ShapeDtypeStruct((ow, oy), BF16),
            jax.ShapeDtypeStruct((2, orows, oy), F32),
        ],
        compiler_params=pltpu.CompilerParams(vmem_limit_bytes=LIMIT),
        name="edges",
    )(state, state, ocean)


def place(index, tiles):
    return (index // tiles, index % tiles)


def my_index(tiles):
    return lax.axis_index("comp") * tiles + lax.axis_index("tile")


def greet_all(n, tiles, me):
    barrier = pltpu.get_barrier_semaphore()

    def signal(d, carry):
        pl.semaphore_signal(barrier, inc=1, device_id=place((me + d) % n, tiles), device_id_type=MESH)
        return carry

    lax.fori_loop(1, n, signal, 0)
    pl.semaphore_wait(barrier, n - 1)


def first_exchange_kernel(n, tiles, sst_ref, edge_ref, xe_ref, st_ref, oc_ref, sea_ref, flux_ref, v_ref,
                          all_ref, halo_ref, xs_ref, ocean_ref, ohalo, ssem, rsem, hs, hr, local):
    me = my_index(tiles)
    east = place((me + 1) % n, tiles)
    west = place((me + n - 1) % n, tiles)
    g = pl.program_id(0)

    def copy(d):
        return pltpu.make_async_remote_copy(
            src_ref=sst_ref, dst_ref=all_ref.at[me], send_sem=ssem.at[d], recv_sem=rsem.at[d],
            device_id=place((me + d) % n, tiles), device_id_type=MESH)

    moves = [
        (xe_ref.at[1], halo_ref.at[0], east),
        (xe_ref.at[0], halo_ref.at[1], west),
        (edge_ref.at[1], ohalo.at[0], east),
        (edge_ref.at[0], ohalo.at[1], west),
    ]
    copies = [
        pltpu.make_async_remote_copy(
            src_ref=s, dst_ref=d, send_sem=hs.at[i], recv_sem=hr.at[i], device_id=to, device_id_type=MESH)
        for i, (s, d, to) in enumerate(moves)
    ]
    own = pltpu.make_async_copy(sst_ref, all_ref.at[me], local)
    width = oc_ref.shape[1]
    columns = st_ref.shape[2]

    @pl.when(g == 0)
    def _():
        greet_all(n, tiles, me)

        def start(d, carry):
            copy(d).start()
            return carry

        lax.fori_loop(1, n, start, 0)
        for c in copies:
            c.start()
        own.start()

    swap = swap_matrix()
    for rb in range(st_ref.shape[0] // G):
        block = st_ref[rb * G : (rb + 1) * G].reshape(G * G, columns)
        xs_ref[:, rb * G : (rb + 1) * G, :] = dot(swap, block).astype(BF16).reshape(G, G, columns)

    @pl.when(g == 0)
    def _():
        ocean_columns(range(1, width - 1), oc_ref, ohalo, sea_ref, flux_ref, v_ref, ocean_ref)

    @pl.when(g == pl.num_programs(0) - 1)
    def _():
        for c in copies:
            c.wait()
        ocean_columns((0, width - 1), oc_ref, ohalo, sea_ref, flux_ref, v_ref, ocean_ref)
        own.wait()

        def finish(d, carry):
            copy(d).wait()
            return carry

        lax.fori_loop(1, n, finish, 0)


def first_exchange(n, tiles, sst, edge, xe, state, ocean, sea, flux, vertical):
    rows, width, cols = state.shape
    dma = pltpu.SemaphoreType.DMA
    return pl.pallas_call(
        functools.partial(first_exchange_kernel, n, tiles),
        grid=(width // G,),
        in_specs=[HBM, HBM, HBM, pl.BlockSpec((rows, G, cols), lambda g: (0, g, 0))]
        + [whole(a.shape) for a in (ocean, sea, flux, vertical)],
        out_specs=[HBM, HBM, pl.BlockSpec((G, rows, cols), lambda g: (g, 0, 0)), whole(ocean.shape)],
        out_shape=[
            jax.ShapeDtypeStruct((n,) + sst.shape, BF16),
            jax.ShapeDtypeStruct((2, rows, cols), BF16),
            jax.ShapeDtypeStruct((width, rows, cols), BF16),
            jax.ShapeDtypeStruct(ocean.shape, F32),
        ],
        scratch_shapes=[pltpu.VMEM(edge.shape, F32), dma((n,)), dma((n,)), dma((4,)), dma((4,)), dma],
        compiler_params=pltpu.CompilerParams(collective_id=0, has_side_effects=True, vmem_limit_bytes=LIMIT),
        name="first_exchange",
    )(sst, edge, xe, state, ocean, sea, flux, vertical)


def halo_exchange_kernel(n, tiles, xs_ref, halo_ref, hs, hr):
    me = my_index(tiles)
    east = place((me + 1) % n, tiles)
    west = place((me + n - 1) % n, tiles)
    barrier = pltpu.get_barrier_semaphore()
    for to in (east, west):
        pl.semaphore_signal(barrier, inc=1, device_id=to, device_id_type=MESH)
    pl.semaphore_wait(barrier, 2)
    width = xs_ref.shape[0]
    copies = [
        pltpu.make_async_remote_copy(
            src_ref=xs_ref.at[s], dst_ref=halo_ref.at[i], send_sem=hs.at[i], recv_sem=hr.at[i],
            device_id=to, device_id_type=MESH)
        for i, (s, to) in enumerate(((width - 1, east), (0, west)))
    ]
    for c in copies:
        c.start()
    for c in copies:
        c.wait()


def halo_exchange(n, tiles, xs):
    width, rows, cols = xs.shape
    dma = pltpu.SemaphoreType.DMA
    return pl.pallas_call(
        functools.partial(halo_exchange_kernel, n, tiles),
        in_specs=[HBM],
        out_specs=HBM,
        out_shape=jax.ShapeDtypeStruct((2, rows, cols), BF16),
        scratch_shapes=[dma((2,)), dma((2,))],
        compiler_params=pltpu.CompilerParams(collective_id=1, has_side_effects=True, vmem_limit_bytes=LIMIT),
        name="halo_exchange",
    )(xs)


def one_hot(owner_ref, block_ref, k, count, per):
    target = owner_ref[k : k + 1, :] * per + block_ref[k : k + 1, :]
    return (iota((count, target.shape[1]), 0) == target).astype(F32).astype(BF16)


def slab_update(xs_ref, halo_ref, x, first, last, cr, lateral):
    width = xs_ref.shape[0]
    center = xs_ref[x]
    west = xs_ref[jnp.maximum(x - 1, 0)]
    east = xs_ref[jnp.minimum(x + 1, width - 1)]
    if first:
        west = jnp.where(x == 0, halo_ref[0], west)
    if last:
        east = jnp.where(x == width - 1, halo_ref[1], east)
    sides = dot(center, lateral) + east.astype(F32)
    return (
        (1.0 - 4.0 * ATM_DIFFUSION - cr) * center.astype(F32)
        + (cr + ATM_DIFFUSION) * west.astype(F32)
        + ATM_DIFFUSION * sides
    )


def force(updated, f_ref, heat, moist):
    rows = updated.shape[0]
    half = rows // 2
    f_ref[...] = updated.astype(BF16)
    last = iota((G, 1), 0) == G - 1
    for end, added in ((half, heat), (rows, moist)):
        part = updated[end - G : end]
        f_ref[end - G : end, :] = jnp.where(last, part + added, part).astype(BF16)


def step_one_kernel(xs_ref, halo_ref, all_ref, owner_ref, block_ref, w_ref, sea_ref, cr_ref, v_ref,
                    new_ref, temp_ref, heat_ref, moist_ref, r0_ref, r1_ref, fetched, forced):
    g = pl.program_id(0)
    xg = new_ref.shape[0]
    jg, kk, block, _ = w_ref.shape
    count = all_ref.shape[0] * all_ref.shape[1]

    @pl.when(g == 0)
    def _():
        table = all_ref[...].reshape(count, block)
        for k in range(kk):
            hot = one_hot(owner_ref, block_ref, k, count, all_ref.shape[1])
            fetched[k] = dot_tn(hot, table).astype(BF16)

    rows = xs_ref.shape[1]
    half = rows // 2
    lateral = lateral_matrix(xs_ref.shape[2])
    vertical = v_ref[...]
    cr = cr_ref[...]
    j0 = pl.multiple_of(g * jg, jg)
    sources = [fetched[k, pl.ds(j0, jg), :] for k in range(kk)]
    per = jg // xg
    for i in range(xg):
        temps = []
        for j in range(per * i, per * i + per):
            total = dot_nt(sources[0], w_ref[j, 0])
            for k in range(1, kk):
                total = total + dot_nt(sources[k], w_ref[j, k])
            temps.append(total[j : j + 1])
        temp = jnp.concatenate(temps, axis=1)
        updated = slab_update(xs_ref, halo_ref, g * xg + i, i == 0, i == xg - 1, cr, lateral)
        sea = EXCHANGE_RATE * sea_ref[i : i + 1, :].astype(F32)
        heat = sea * (temp - updated[half - 1 : half])
        moist = sea * (0.5 * temp - updated[rows - 1 : rows])
        slot = forced.at[i % 2]
        force(updated, slot, heat, moist)
        mixed = dot(vertical, slot[...]).astype(BF16)
        new_ref[i] = mixed
        temp_ref[i : i + 1, :] = temp
        heat_ref[i : i + 1, :] = heat
        moist_ref[i : i + 1, :] = moist
        r0_ref[i : i + 1, :] = mixed[half - G : half].astype(F32)[G - 1 : G]
        r1_ref[i : i + 1, :] = mixed[rows - G : rows].astype(F32)[G - 1 : G]


def whole(shape):
    return pl.BlockSpec(shape, lambda g: (0,) * len(shape))


def step_one(xs, halo, all_sst, owner, blocks, weight, sea, cr, vertical):
    width, rows, cols = xs.shape
    jb, kk, block, _ = weight.shape
    xg = 8
    steps = width // xg
    jg = jb // steps
    row = pl.BlockSpec((xg, cols), lambda g: (g, 0))
    rowshape = jax.ShapeDtypeStruct((width, cols), F32)
    return pl.pallas_call(
        step_one_kernel,
        grid=(steps,),
        in_specs=[
            whole(xs.shape), whole(halo.shape), whole(all_sst.shape), whole(owner.shape), whole(blocks.shape),
            pl.BlockSpec((jg, kk, block, block), lambda g: (g, 0, 0, 0)),
            row, whole(cr.shape), whole(vertical.shape),
        ],
        out_specs=[pl.BlockSpec((xg, rows, cols), lambda g: (g, 0, 0))] + [row] * 5,
        out_shape=[jax.ShapeDtypeStruct(xs.shape, BF16)] + [rowshape] * 5,
        scratch_shapes=[pltpu.VMEM((kk, jb, block), BF16), pltpu.VMEM((2, rows, cols), BF16)],
        compiler_params=pltpu.CompilerParams(vmem_limit_bytes=LIMIT),
        name="step_one",
    )(xs, halo, all_sst, owner, blocks, weight, sea, cr, vertical)


def push_kernel(r0_ref, r1_ref, halo_ref, cr_ref, sea_ref, temp_ref, heat_ref, moist_ref, owner_ref, block_ref, w_ref,
                heat2_ref, moist2_ref, acc_ref, mean, shares):
    g = pl.program_id(0)
    width, cols = r0_ref.shape
    jg, kk, block, _ = w_ref.shape
    rows = halo_ref.shape[1]
    per_owner = acc_ref.shape[1]

    @pl.when(g == 0)
    def _():
        lateral = lateral_matrix(cols)
        sea = EXCHANGE_RATE * sea_ref[...].astype(F32)
        temp = temp_ref[...]
        for v, (ref, end, gain, old, out) in enumerate((
            (r0_ref, rows // 2, 1.0, heat_ref, heat2_ref),
            (r1_ref, rows, 0.5, moist_ref, moist2_ref),
        )):
            center = ref[...]
            hw = halo_ref[0, end - G : end, :].astype(F32)[G - 1 : G]
            he = halo_ref[1, end - G : end, :].astype(F32)[G - 1 : G]
            west = jnp.concatenate([hw, center[:-1]], axis=0)
            east = jnp.concatenate([center[1:], he], axis=0)
            cr = cr_ref[end - 1 : end, :]
            updated = (
                (1.0 - 4.0 * ATM_DIFFUSION - cr) * center
                + (cr + ATM_DIFFUSION) * west
                + ATM_DIFFUSION * (dot(center.astype(BF16), lateral) + east)
            )
            flux = sea * (gain * temp - updated)
            out[...] = flux
            mean[v] = (0.5 * old[...] + 0.5 * flux).astype(BF16).astype(F32)

    xg = width * jg // owner_ref.shape[1]
    per = jg // xg
    x0 = pl.multiple_of(g * xg, xg)
    lefts = [
        jnp.concatenate([mean[v, pl.ds(x0, xg), h * block : (h + 1) * block] for v in range(2)], axis=0).astype(BF16)
        for h in range(per)
    ]
    j0 = pl.multiple_of(g * jg, jg)
    for k in range(kk):
        rows_of = []
        for j in range(jg):
            i = j // per
            share = dot(lefts[j % per], w_ref[j, k])
            rows_of.append(jnp.concatenate([share[i : i + 1], share[xg + i : xg + i + 1]], axis=1))
        shares[k, pl.ds(j0, jg), :] = jnp.concatenate(rows_of, axis=0)

    @pl.when(g == pl.num_programs(0) - 1)
    def _():
        count = acc_ref.shape[0] * per_owner
        total = jnp.zeros((count, 2 * block), F32)
        for k in range(kk):
            hot = one_hot(owner_ref, block_ref, k, count, per_owner)
            share = shares[k]
            high = share.astype(BF16)
            low = (share - high.astype(F32)).astype(BF16)
            total = total + dot(hot, high) + dot(hot, low)
        acc_ref[...] = total.astype(BF16).reshape(acc_ref.shape)


def push(n, per_owner, r0, r1, halo, cr, sea, temp, heat, moist, owner, blocks, weight):
    width, cols = r0.shape
    jb, kk, block, _ = weight.shape
    steps = width // 8
    jg = jb // steps
    return pl.pallas_call(
        push_kernel,
        grid=(steps,),
        in_specs=[whole(a.shape) for a in (r0, r1, halo, cr, sea, temp, heat, moist, owner, blocks)]
        + [pl.BlockSpec((jg, kk, block, block), lambda g: (g, 0, 0, 0))],
        out_specs=[whole(r0.shape), whole(r0.shape), whole((n, per_owner, 2 * block))],
        out_shape=[
            jax.ShapeDtypeStruct(r0.shape, F32),
            jax.ShapeDtypeStruct(r0.shape, F32),
            jax.ShapeDtypeStruct((n, per_owner, 2 * block), BF16),
        ],
        scratch_shapes=[pltpu.VMEM((2, width, cols), F32), pltpu.VMEM((kk, jb, 2 * block), F32)],
        compiler_params=pltpu.CompilerParams(vmem_limit_bytes=LIMIT),
        name="push",
    )(r0, r1, halo, cr, sea, temp, heat, moist, owner, blocks, weight)


def step_two_kernel(n, tiles, acc_ref, osea_ref, xs_ref, halo_ref, heat_ref, moist_ref, cr_ref, v_ref,
                    out_ref, flux_ref, forced, new, land, ssem, rsem, local):
    me = my_index(tiles)
    g = pl.program_id(0)

    def copy(d):
        to = (me + d) % n
        return pltpu.make_async_remote_copy(
            src_ref=acc_ref.at[to], dst_ref=land.at[d], send_sem=ssem.at[d], recv_sem=rsem.at[d],
            device_id=place(to, tiles), device_id_type=MESH)

    own = pltpu.make_async_copy(acc_ref.at[me], land.at[0], local)

    @pl.when(g == 0)
    def _():
        greet_all(n, tiles, me)

        def start(d, carry):
            copy(d).start()
            return carry

        lax.fori_loop(1, n, start, 0)
        own.start()

    cols = xs_ref.shape[2]
    lateral = lateral_matrix(cols)
    swap = swap_matrix()
    vertical = v_ref[...]
    cr = cr_ref[...]
    for i in range(G):
        updated = slab_update(xs_ref, halo_ref, g * G + i, i == 0, i == G - 1, cr, lateral)
        slot = forced.at[i % 2]
        force(updated, slot, heat_ref[i : i + 1, :], moist_ref[i : i + 1, :])
        new[i] = dot(vertical, slot[...]).astype(BF16)
    for rb in range(out_ref.shape[0] // G):
        block = new[:, rb * G : (rb + 1) * G, :].reshape(G * G, cols)
        out_ref[rb * G : (rb + 1) * G] = dot(swap, block).astype(BF16).reshape(G, G, cols)

    @pl.when(g == pl.num_programs(0) - 1)
    def _():
        own.wait()

        def finish(d, total):
            copy(d).wait()
            return total + land[d].astype(F32)

        total = lax.fori_loop(1, n, finish, land[0].astype(F32))
        sea = osea_ref[...].astype(F32)
        block = sea.shape[1]
        flux_ref[0] = total[:, :block] * sea
        flux_ref[1] = total[:, block:] * sea


def step_two(n, tiles, acc, osea, xs, halo, heat, moist, cr, vertical):
    width, rows, cols = xs.shape
    dma = pltpu.SemaphoreType.DMA
    row = pl.BlockSpec((G, cols), lambda g: (g, 0))
    return pl.pallas_call(
        functools.partial(step_two_kernel, n, tiles),
        grid=(width // G,),
        in_specs=[HBM, whole(osea.shape), whole(xs.shape), whole(halo.shape), row, row, whole(cr.shape),
                  whole(vertical.shape)],
        out_specs=[pl.BlockSpec((rows, G, cols), lambda g: (0, g, 0)), whole((2,) + osea.shape)],
        out_shape=[
            jax.ShapeDtypeStruct((rows, width, cols), BF16),
            jax.ShapeDtypeStruct((2,) + osea.shape, F32),
        ],
        scratch_shapes=[
            pltpu.VMEM((2, rows, cols), BF16), pltpu.VMEM((G, rows, cols), BF16), pltpu.VMEM(acc.shape, BF16),
            dma((n,)), dma((n,)), dma,
        ],
        compiler_params=pltpu.CompilerParams(collective_id=2, has_side_effects=True, vmem_limit_bytes=LIMIT),
        name="step_two",
    )(acc, osea, xs, halo, heat, moist, cr, vertical)


def ocean_columns(columns, oc_ref, halo_ref, sea_ref, flux_ref, v_ref, out_ref):
    rows, width, cols = oc_ref.shape
    half = rows // 2
    vertical = v_ref[...]
    vhigh = vertical.astype(BF16)
    vlow = (vertical - vhigh.astype(F32)).astype(BF16)
    lane = iota((1, cols), 1)
    row = iota((rows, 1), 0)
    for x in columns:
        center = oc_ref[:, x, :]
        west = halo_ref[0] if x == 0 else oc_ref[:, x - 1, :]
        east = halo_ref[1] if x == width - 1 else oc_ref[:, x + 1, :]
        north = jnp.where(lane == cols - 1, center, pltpu.roll(center, cols - 1, 1))
        south = jnp.where(lane == 0, center, pltpu.roll(center, 1, 1))
        tendency = east + west + (north + south) - 4.0 * center
        sea = sea_ref[x : x + 1, :].astype(F32)
        heat = FLUX_GAIN * sea * flux_ref[0, x : x + 1, :]
        fresh = FLUX_GAIN * sea * flux_ref[1, x : x + 1, :]
        updated = (center + OCEAN_DIFFUSION * tendency) * sea
        updated = updated + jnp.where(row == 0, heat, jnp.where(row == half, fresh, 0.0))
        high = updated.astype(BF16)
        low = (updated - high.astype(F32)).astype(BF16)
        mixed = dot(vhigh, high) + (dot(vhigh, low) + dot(vlow, high))
        out_ref[:, x, :] = mixed


def per_device(n, tiles, atm_state, atm_sea, zonal_courant, atm_vertical, ocean_state, ocean_sea, flux_in,
               ocean_vertical, remap_owner, remap_block, remap_weight):
    owner = remap_owner.T
    blocks = remap_block.T
    cr = zonal_courant.reshape(-1, 1)
    xe, sst, edge = edges(atm_state, ocean_state)
    all_sst, halo, xs, ocean_next = first_exchange(
        n, tiles, sst, edge, xe, atm_state, ocean_state, ocean_sea, flux_in, ocean_vertical)
    new, temp, heat, moist, r0, r1 = step_one(
        xs, halo, all_sst, owner, blocks, remap_weight, atm_sea, cr, atm_vertical)
    halo2 = halo_exchange(n, tiles, new)
    heat2, moist2, acc = push(
        n, sst.shape[0], r0, r1, halo2, cr, atm_sea, temp, heat, moist, owner, blocks, remap_weight)
    atm_next, ocean_flux = step_two(n, tiles, acc, ocean_sea, new, halo2, heat2, moist2, cr, atm_vertical)
    return atm_next, ocean_next, ocean_flux


def solution(mesh):
    tiles = mesh.shape["tile"]
    n = mesh.shape["comp"] * tiles
    return jax.shard_map(
        functools.partial(per_device, n, tiles),
        mesh=mesh,
        in_specs=(
            P(None, AXES, None), P(AXES, None), P(), P(), P(None, AXES, None), P(AXES, None),
            P(None, AXES, None), P(), P(AXES, None), P(AXES, None), P(AXES, None, None, None),
        ),
        out_specs=(P(None, AXES, None), P(None, AXES, None), P(None, AXES, None)),
        check_vma=False,
    )
```

```python
import functools

import jax
import jax.numpy as jnp
from jax import lax
from jax.experimental import pallas as pl
from jax.experimental.pallas import tpu as pltpu
from jax.sharding import PartitionSpec as P

ATM_DIFFUSION = 0.1
OCEAN_DIFFUSION = 0.15
EXCHANGE_RATE = 0.3
FLUX_GAIN = 0.5
MESH = pl.DeviceIdType.MESH
AXES = ("comp", "tile")
F32 = jnp.float32
BF16 = jnp.bfloat16
G = 16
HBM = pl.BlockSpec(memory_space=pltpu.HBM)
LIMIT = 60 * 1024 * 1024


def iota(shape, dim):
    return lax.broadcasted_iota(jnp.int32, shape, dim)


def swap_matrix():
    a = iota((G * G, G * G), 0)
    b = iota((G * G, G * G), 1)
    return ((a // G == b % G) & (a % G == b // G)).astype(F32).astype(BF16)


def lateral_matrix(n):
    a = iota((n, n), 0)
    b = iota((n, n), 1)
    north = a == jnp.minimum(b + 1, n - 1)
    south = a == jnp.maximum(b - 1, 0)
    return (north.astype(F32) + south.astype(F32)).astype(BF16)


def dot(a, b):
    return jnp.dot(a, b, preferred_element_type=F32)


def dot_nt(a, b):
    return lax.dot_general(a, b, (((1,), (1,)), ((), ())), preferred_element_type=F32)


def dot_tn(a, b):
    return lax.dot_general(a, b, (((0,), (0,)), ((), ())), preferred_element_type=F32)


def edges_kernel(lo_ref, hi_ref, oc_ref, courant_ref, xe_ref, sst_ref, edge_ref, cr_ref):
    order = courant_ref.shape[1]
    diagonal = iota((order, order), 0) == iota((order, order), 1)
    cr_ref[...] = jnp.sum(jnp.where(diagonal, courant_ref[...], 0.0), axis=1, keepdims=True)
    width = oc_ref.shape[1]
    part = hi_ref.shape[1]
    sst_ref[...] = oc_ref[0].astype(BF16)
    edge_ref[0] = oc_ref[:, 0, :]
    edge_ref[1] = oc_ref[:, width - 1, :]
    swap = swap_matrix()
    picks = (swap[:G], swap[G * G - G :])
    cols = lo_ref.shape[2]
    for rb in range(lo_ref.shape[0] // G):
        for side, ref in enumerate((lo_ref, hi_ref)):
            block = ref[rb * G : (rb + 1) * G].reshape(G * part, cols)
            xe_ref[side, rb * G : (rb + 1) * G, :] = dot(picks[side], block).astype(BF16)


def edges(state, ocean, courant):
    rows, width, cols = state.shape
    orows, ow, oy = ocean.shape
    last = width // G - 1
    return pl.pallas_call(
        edges_kernel,
        grid=(1,),
        in_specs=[
            pl.BlockSpec((rows, G, cols), lambda g: (0, 0, 0)),
            pl.BlockSpec((rows, G, cols), lambda g: (0, last, 0)),
            pl.BlockSpec((orows, ow, oy), lambda g: (0, 0, 0)),
            pl.BlockSpec((1, rows), lambda g: (0, 0)),
        ],
        out_specs=[
            pl.BlockSpec((2, rows, cols), lambda g: (0, 0, 0)),
            pl.BlockSpec((ow, oy), lambda g: (0, 0)),
            pl.BlockSpec((2, orows, oy), lambda g: (0, 0, 0)),
            pl.BlockSpec((rows, 1), lambda g: (0, 0)),
        ],
        out_shape=[
            jax.ShapeDtypeStruct((2, rows, cols), BF16),
            jax.ShapeDtypeStruct((ow, oy), BF16),
            jax.ShapeDtypeStruct((2, orows, oy), F32),
            jax.ShapeDtypeStruct((rows, 1), F32),
        ],
        compiler_params=pltpu.CompilerParams(vmem_limit_bytes=LIMIT),
        name="edges",
    )(state, state, ocean, courant)


def place(index, tiles):
    return (index // tiles, index % tiles)


def my_index(tiles):
    return lax.axis_index("comp") * tiles + lax.axis_index("tile")


def greet_all(n, tiles, me):
    barrier = pltpu.get_barrier_semaphore()

    def signal(d, carry):
        pl.semaphore_signal(barrier, inc=1, device_id=place((me + d) % n, tiles), device_id_type=MESH)
        return carry

    lax.fori_loop(1, n, signal, 0)
    pl.semaphore_wait(barrier, n - 1)


def first_exchange_kernel(n, tiles, sst_ref, edge_ref, xe_ref, st_ref, oc_ref, sea_ref, flux_ref, v_ref,
                          all_ref, halo_ref, xs_ref, ocean_ref, ohalo, ssem, rsem, hs, hr, local):
    me = my_index(tiles)
    east = place((me + 1) % n, tiles)
    west = place((me + n - 1) % n, tiles)
    g = pl.program_id(0)

    def copy(d):
        return pltpu.make_async_remote_copy(
            src_ref=sst_ref, dst_ref=all_ref.at[me], send_sem=ssem.at[d], recv_sem=rsem.at[d],
            device_id=place((me + d) % n, tiles), device_id_type=MESH)

    moves = [
        (xe_ref.at[1], halo_ref.at[0], east),
        (xe_ref.at[0], halo_ref.at[1], west),
        (edge_ref.at[1], ohalo.at[0], east),
        (edge_ref.at[0], ohalo.at[1], west),
    ]
    copies = [
        pltpu.make_async_remote_copy(
            src_ref=s, dst_ref=d, send_sem=hs.at[i], recv_sem=hr.at[i], device_id=to, device_id_type=MESH)
        for i, (s, d, to) in enumerate(moves)
    ]
    own = pltpu.make_async_copy(sst_ref, all_ref.at[me], local)
    width = oc_ref.shape[1]
    columns = st_ref.shape[2]

    @pl.when(g == 0)
    def _():
        greet_all(n, tiles, me)

        def start(d, carry):
            copy(d).start()
            return carry

        lax.fori_loop(1, n, start, 0)
        for c in copies:
            c.start()
        own.start()

    swap = swap_matrix()
    for rb in range(st_ref.shape[0] // G):
        block = st_ref[rb * G : (rb + 1) * G].reshape(G * G, columns)
        xs_ref[:, rb * G : (rb + 1) * G, :] = dot(swap, block).astype(BF16).reshape(G, G, columns)

    @pl.when(g == 0)
    def _():
        ocean_columns(range(1, width - 1), oc_ref, ohalo, sea_ref, flux_ref, v_ref, ocean_ref)

    @pl.when(g == pl.num_programs(0) - 1)
    def _():
        for c in copies:
            c.wait()
        ocean_columns((0, width - 1), oc_ref, ohalo, sea_ref, flux_ref, v_ref, ocean_ref)
        own.wait()

        def finish(d, carry):
            copy(d).wait()
            return carry

        lax.fori_loop(1, n, finish, 0)


def first_exchange(n, tiles, sst, edge, xe, state, ocean, sea, flux, vertical):
    rows, width, cols = state.shape
    dma = pltpu.SemaphoreType.DMA
    return pl.pallas_call(
        functools.partial(first_exchange_kernel, n, tiles),
        grid=(width // G,),
        in_specs=[HBM, HBM, HBM, pl.BlockSpec((rows, G, cols), lambda g: (0, g, 0))]
        + [whole(a.shape) for a in (ocean, sea, flux, vertical)],
        out_specs=[HBM, HBM, pl.BlockSpec((G, rows, cols), lambda g: (g, 0, 0)), whole(ocean.shape)],
        out_shape=[
            jax.ShapeDtypeStruct((n,) + sst.shape, BF16),
            jax.ShapeDtypeStruct((2, rows, cols), BF16),
            jax.ShapeDtypeStruct((width, rows, cols), BF16),
            jax.ShapeDtypeStruct(ocean.shape, F32),
        ],
        scratch_shapes=[pltpu.VMEM(edge.shape, F32), dma((n,)), dma((n,)), dma((4,)), dma((4,)), dma],
        compiler_params=pltpu.CompilerParams(collective_id=0, has_side_effects=True, vmem_limit_bytes=LIMIT),
        name="first_exchange",
    )(sst, edge, xe, state, ocean, sea, flux, vertical)


def one_hot(owner_ref, block_ref, k, count, per):
    target = owner_ref[k : k + 1, :] * per + block_ref[k : k + 1, :]
    return (iota((count, target.shape[1]), 0) == target).astype(F32).astype(BF16)


def slab_update(xs_ref, halo_ref, x, first, last, cr, lateral):
    width = xs_ref.shape[0]
    center = xs_ref[x]
    west = xs_ref[jnp.maximum(x - 1, 0)]
    east = xs_ref[jnp.minimum(x + 1, width - 1)]
    if first:
        west = jnp.where(x == 0, halo_ref[0], west)
    if last:
        east = jnp.where(x == width - 1, halo_ref[1], east)
    sides = dot(center, lateral) + east.astype(F32)
    return (
        (1.0 - 4.0 * ATM_DIFFUSION - cr) * center.astype(F32)
        + (cr + ATM_DIFFUSION) * west.astype(F32)
        + ATM_DIFFUSION * sides
    )


def force(updated, f_ref, heat, moist):
    rows = updated.shape[0]
    half = rows // 2
    f_ref[...] = updated.astype(BF16)
    last = iota((G, 1), 0) == G - 1
    for end, added in ((half, heat), (rows, moist)):
        part = updated[end - G : end]
        f_ref[end - G : end, :] = jnp.where(last, part + added, part).astype(BF16)


def step_one_kernel(n, tiles, xs_ref, halo_ref, all_ref, owner_ref, block_ref, w_ref, sea_ref, cr_ref, v_ref,
                    new_ref, temp_ref, heat_ref, moist_ref, r0_ref, r1_ref, halo2_ref, fetched, forced, ends, hs, hr):
    step = pl.program_id(0)
    steps = pl.num_programs(0)
    g = (step + steps - 1) % steps
    me = my_index(tiles)
    east = place((me + 1) % n, tiles)
    west = place((me + n - 1) % n, tiles)
    copies = [
        pltpu.make_async_remote_copy(
            src_ref=ends.at[i], dst_ref=halo2_ref.at[i], send_sem=hs.at[i], recv_sem=hr.at[i],
            device_id=to, device_id_type=MESH)
        for i, to in enumerate((east, west))
    ]

    @pl.when(step == 0)
    def _():
        barrier = pltpu.get_barrier_semaphore()
        for to in (east, west):
            pl.semaphore_signal(barrier, inc=1, device_id=to, device_id_type=MESH)
        pl.semaphore_wait(barrier, 2)

    for i in range(2):

        @pl.when(step == i + 1)
        def _():
            copies[i].start()

    xg = new_ref.shape[0]
    jg, kk, block, _ = w_ref.shape
    count = all_ref.shape[0] * all_ref.shape[1]

    @pl.when(step == 0)
    def _():
        table = all_ref[...].reshape(count, block)
        for k in range(kk):
            hot = one_hot(owner_ref, block_ref, k, count, all_ref.shape[1])
            fetched[k] = dot_tn(hot, table).astype(BF16)

    rows = xs_ref.shape[1]
    half = rows // 2
    lateral = lateral_matrix(xs_ref.shape[2])
    vertical = v_ref[...]
    cr = cr_ref[...]
    j0 = pl.multiple_of(g * jg, jg)
    sources = [fetched[k, pl.ds(j0, jg), :] for k in range(kk)]
    per = jg // xg
    for i in range(xg):
        temps = []
        for j in range(per * i, per * i + per):
            total = dot_nt(sources[0], w_ref[j, 0])
            for k in range(1, kk):
                total = total + dot_nt(sources[k], w_ref[j, k])
            temps.append(total[j : j + 1])
        temp = jnp.concatenate(temps, axis=1)
        updated = slab_update(xs_ref, halo_ref, g * xg + i, i == 0, i == xg - 1, cr, lateral)
        sea = EXCHANGE_RATE * sea_ref[i : i + 1, :].astype(F32)
        heat = sea * (temp - updated[half - 1 : half])
        moist = sea * (0.5 * temp - updated[rows - 1 : rows])
        slot = forced.at[i % 2]
        force(updated, slot, heat, moist)
        mixed = dot(vertical, slot[...]).astype(BF16)
        new_ref[i] = mixed
        temp_ref[i : i + 1, :] = temp
        heat_ref[i : i + 1, :] = heat
        moist_ref[i : i + 1, :] = moist
        r0_ref[i : i + 1, :] = mixed[half - G : half].astype(F32)[G - 1 : G]
        r1_ref[i : i + 1, :] = mixed[rows - G : rows].astype(F32)[G - 1 : G]

    @pl.when(step == 0)
    def _():
        ends[0] = new_ref[xg - 1]

    @pl.when(step == 1)
    def _():
        ends[1] = new_ref[0]

    @pl.when(step == steps - 1)
    def _():
        for c in copies:
            c.wait()


def whole(shape):
    return pl.BlockSpec(shape, lambda g: (0,) * len(shape))


def step_one(n, tiles, xs, halo, all_sst, owner, blocks, weight, sea, cr, vertical):
    width, rows, cols = xs.shape
    jb, kk, block, _ = weight.shape
    xg = 8
    steps = width // xg
    jg = jb // steps
    dma = pltpu.SemaphoreType.DMA

    def turn(g):
        return (g + steps - 1) % steps

    row = pl.BlockSpec((xg, cols), lambda g: (turn(g), 0))
    rowshape = jax.ShapeDtypeStruct((width, cols), F32)
    return pl.pallas_call(
        functools.partial(step_one_kernel, n, tiles),
        grid=(steps,),
        in_specs=[
            whole(xs.shape), whole(halo.shape), whole(all_sst.shape), whole(owner.shape), whole(blocks.shape),
            pl.BlockSpec((jg, kk, block, block), lambda g: (turn(g), 0, 0, 0)),
            row, whole(cr.shape), whole(vertical.shape),
        ],
        out_specs=[pl.BlockSpec((xg, rows, cols), lambda g: (turn(g), 0, 0))] + [row] * 5 + [HBM],
        out_shape=[jax.ShapeDtypeStruct(xs.shape, BF16)] + [rowshape] * 5 + [jax.ShapeDtypeStruct(halo.shape, BF16)],
        scratch_shapes=[
            pltpu.VMEM((kk, jb, block), BF16), pltpu.VMEM((2, rows, cols), BF16), pltpu.VMEM((2, rows, cols), BF16),
            dma((2,)), dma((2,)),
        ],
        compiler_params=pltpu.CompilerParams(collective_id=1, has_side_effects=True, vmem_limit_bytes=LIMIT),
        name="step_one",
    )(xs, halo, all_sst, owner, blocks, weight, sea, cr, vertical)


def push_kernel(r0_ref, r1_ref, halo_ref, cr_ref, sea_ref, temp_ref, heat_ref, moist_ref, owner_ref, block_ref, w_ref,
                heat2_ref, moist2_ref, acc_ref, mean, shares):
    g = pl.program_id(0)
    width, cols = r0_ref.shape
    jg, kk, block, _ = w_ref.shape
    rows = halo_ref.shape[1]
    per_owner = acc_ref.shape[1]

    @pl.when(g == 0)
    def _():
        lateral = lateral_matrix(cols)
        sea = EXCHANGE_RATE * sea_ref[...].astype(F32)
        temp = temp_ref[...]
        for v, (ref, end, gain, old, out) in enumerate((
            (r0_ref, rows // 2, 1.0, heat_ref, heat2_ref),
            (r1_ref, rows, 0.5, moist_ref, moist2_ref),
        )):
            center = ref[...]
            hw = halo_ref[0, end - G : end, :].astype(F32)[G - 1 : G]
            he = halo_ref[1, end - G : end, :].astype(F32)[G - 1 : G]
            west = jnp.concatenate([hw, center[:-1]], axis=0)
            east = jnp.concatenate([center[1:], he], axis=0)
            cr = cr_ref[end - 1 : end, :]
            updated = (
                (1.0 - 4.0 * ATM_DIFFUSION - cr) * center
                + (cr + ATM_DIFFUSION) * west
                + ATM_DIFFUSION * (dot(center.astype(BF16), lateral) + east)
            )
            flux = sea * (gain * temp - updated)
            out[...] = flux
            mean[v] = (0.5 * old[...] + 0.5 * flux).astype(BF16).astype(F32)

    xg = width * jg // owner_ref.shape[1]
    per = jg // xg
    x0 = pl.multiple_of(g * xg, xg)
    lefts = [
        jnp.concatenate([mean[v, pl.ds(x0, xg), h * block : (h + 1) * block] for v in range(2)], axis=0).astype(BF16)
        for h in range(per)
    ]
    j0 = pl.multiple_of(g * jg, jg)
    for k in range(kk):
        rows_of = []
        for j in range(jg):
            i = j // per
            share = dot(lefts[j % per], w_ref[j, k])
            rows_of.append(jnp.concatenate([share[i : i + 1], share[xg + i : xg + i + 1]], axis=1))
        shares[k, pl.ds(j0, jg), :] = jnp.concatenate(rows_of, axis=0)

    @pl.when(g == pl.num_programs(0) - 1)
    def _():
        count = acc_ref.shape[0] * per_owner
        total = jnp.zeros((count, 2 * block), F32)
        for k in range(kk):
            hot = one_hot(owner_ref, block_ref, k, count, per_owner)
            share = shares[k]
            high = share.astype(BF16)
            low = (share - high.astype(F32)).astype(BF16)
            total = total + dot(hot, high) + dot(hot, low)
        acc_ref[...] = total.astype(BF16).reshape(acc_ref.shape)


def push(n, per_owner, r0, r1, halo, cr, sea, temp, heat, moist, owner, blocks, weight):
    width, cols = r0.shape
    jb, kk, block, _ = weight.shape
    steps = width // 8
    jg = jb // steps
    return pl.pallas_call(
        push_kernel,
        grid=(steps,),
        in_specs=[whole(a.shape) for a in (r0, r1, halo, cr, sea, temp, heat, moist, owner, blocks)]
        + [pl.BlockSpec((jg, kk, block, block), lambda g: (g, 0, 0, 0))],
        out_specs=[whole(r0.shape), whole(r0.shape), whole((n, per_owner, 2 * block))],
        out_shape=[
            jax.ShapeDtypeStruct(r0.shape, F32),
            jax.ShapeDtypeStruct(r0.shape, F32),
            jax.ShapeDtypeStruct((n, per_owner, 2 * block), BF16),
        ],
        scratch_shapes=[pltpu.VMEM((2, width, cols), F32), pltpu.VMEM((kk, jb, 2 * block), F32)],
        compiler_params=pltpu.CompilerParams(vmem_limit_bytes=LIMIT),
        name="push",
    )(r0, r1, halo, cr, sea, temp, heat, moist, owner, blocks, weight)


def step_two_kernel(n, tiles, acc_ref, osea_ref, xs_ref, halo_ref, heat_ref, moist_ref, cr_ref, v_ref,
                    out_ref, flux_ref, forced, land, ssem, rsem, local):
    me = my_index(tiles)
    g = pl.program_id(0)

    def copy(d):
        to = (me + d) % n
        return pltpu.make_async_remote_copy(
            src_ref=acc_ref.at[to], dst_ref=land.at[d], send_sem=ssem.at[d], recv_sem=rsem.at[d],
            device_id=place(to, tiles), device_id_type=MESH)

    own = pltpu.make_async_copy(acc_ref.at[me], land.at[0], local)

    @pl.when(g == 0)
    def _():
        greet_all(n, tiles, me)

        def start(d, carry):
            copy(d).start()
            return carry

        lax.fori_loop(1, n, start, 0)
        own.start()

    cols = xs_ref.shape[2]
    lateral = lateral_matrix(cols)
    vertical = v_ref[...]
    cr = cr_ref[...]
    for i in range(G):
        updated = slab_update(xs_ref, halo_ref, g * G + i, i == 0, i == G - 1, cr, lateral)
        slot = forced.at[i % 2]
        force(updated, slot, heat_ref[i : i + 1, :], moist_ref[i : i + 1, :])
        out_ref[i] = dot(vertical, slot[...]).astype(BF16)

    @pl.when(g == pl.num_programs(0) - 1)
    def _():
        own.wait()

        def finish(d, total):
            copy(d).wait()
            return total + land[d].astype(F32)

        total = lax.fori_loop(1, n, finish, land[0].astype(F32))
        sea = osea_ref[...].astype(F32)
        block = sea.shape[1]
        flux_ref[0] = total[:, :block] * sea
        flux_ref[1] = total[:, block:] * sea


def step_two(n, tiles, acc, osea, xs, halo, heat, moist, cr, vertical):
    width, rows, cols = xs.shape
    dma = pltpu.SemaphoreType.DMA
    row = pl.BlockSpec((G, cols), lambda g: (g, 0))
    return pl.pallas_call(
        functools.partial(step_two_kernel, n, tiles),
        grid=(width // G,),
        in_specs=[HBM, whole(osea.shape), whole(xs.shape), whole(halo.shape), row, row, whole(cr.shape),
                  whole(vertical.shape)],
        out_specs=[pl.BlockSpec((G, rows, cols), lambda g: (g, 0, 0)), whole((2,) + osea.shape)],
        out_shape=[
            jax.ShapeDtypeStruct((width, rows, cols), BF16),
            jax.ShapeDtypeStruct((2,) + osea.shape, F32),
        ],
        scratch_shapes=[
            pltpu.VMEM((2, rows, cols), BF16), pltpu.VMEM(acc.shape, BF16),
            dma((n,)), dma((n,)), dma,
        ],
        compiler_params=pltpu.CompilerParams(collective_id=2, has_side_effects=True, vmem_limit_bytes=LIMIT),
        name="step_two",
    )(acc, osea, xs, halo, heat, moist, cr, vertical)


def restore_kernel(new_ref, out_ref):
    cols = new_ref.shape[2]
    swap = swap_matrix()
    for rb in range(out_ref.shape[0] // G):
        block = new_ref[:, rb * G : (rb + 1) * G, :].reshape(G * G, cols)
        out_ref[rb * G : (rb + 1) * G] = dot(swap, block).astype(BF16).reshape(G, G, cols)


def restore(new):
    width, rows, cols = new.shape
    part = rows // 2
    return pl.pallas_call(
        restore_kernel,
        grid=(2, width // G),
        in_specs=[pl.BlockSpec((G, part, cols), lambda r, g: (g, r, 0))],
        out_specs=pl.BlockSpec((part, G, cols), lambda r, g: (r, g, 0)),
        out_shape=jax.ShapeDtypeStruct((rows, width, cols), BF16),
        compiler_params=pltpu.CompilerParams(vmem_limit_bytes=LIMIT),
        name="restore",
    )(new)


def ocean_columns(columns, oc_ref, halo_ref, sea_ref, flux_ref, v_ref, out_ref):
    rows, width, cols = oc_ref.shape
    half = rows // 2
    vertical = v_ref[...]
    vhigh = vertical.astype(BF16)
    vlow = (vertical - vhigh.astype(F32)).astype(BF16)
    lane = iota((1, cols), 1)
    row = iota((rows, 1), 0)
    for x in columns:
        center = oc_ref[:, x, :]
        west = halo_ref[0] if x == 0 else oc_ref[:, x - 1, :]
        east = halo_ref[1] if x == width - 1 else oc_ref[:, x + 1, :]
        north = jnp.where(lane == cols - 1, center, pltpu.roll(center, cols - 1, 1))
        south = jnp.where(lane == 0, center, pltpu.roll(center, 1, 1))
        tendency = east + west + (north + south) - 4.0 * center
        sea = sea_ref[x : x + 1, :].astype(F32)
        heat = FLUX_GAIN * sea * flux_ref[0, x : x + 1, :]
        fresh = FLUX_GAIN * sea * flux_ref[1, x : x + 1, :]
        updated = (center + OCEAN_DIFFUSION * tendency) * sea
        updated = updated + jnp.where(row == 0, heat, jnp.where(row == half, fresh, 0.0))
        high = updated.astype(BF16)
        low = (updated - high.astype(F32)).astype(BF16)
        mixed = dot(vhigh, high) + (dot(vhigh, low) + dot(vlow, high))
        out_ref[:, x, :] = mixed


def per_device(n, tiles, atm_state, atm_sea, zonal_courant, atm_vertical, ocean_state, ocean_sea, flux_in,
               ocean_vertical, remap_owner, remap_block, remap_weight):
    owner = remap_owner.T
    blocks = remap_block.T
    xe, sst, edge, cr = edges(atm_state, ocean_state, zonal_courant.reshape(1, -1))
    all_sst, halo, xs, ocean_next = first_exchange(
        n, tiles, sst, edge, xe, atm_state, ocean_state, ocean_sea, flux_in, ocean_vertical)
    new, temp, heat, moist, r0, r1, halo2 = step_one(
        n, tiles, xs, halo, all_sst, owner, blocks, remap_weight, atm_sea, cr, atm_vertical)
    heat2, moist2, acc = push(
        n, sst.shape[0], r0, r1, halo2, cr, atm_sea, temp, heat, moist, owner, blocks, remap_weight)
    final, ocean_flux = step_two(n, tiles, acc, ocean_sea, new, halo2, heat2, moist2, cr, atm_vertical)
    return restore(final), ocean_next, ocean_flux


def solution(mesh):
    tiles = mesh.shape["tile"]
    n = mesh.shape["comp"] * tiles
    return jax.shard_map(
        functools.partial(per_device, n, tiles),
        mesh=mesh,
        in_specs=(
            P(None, AXES, None), P(AXES, None), P(), P(), P(None, AXES, None), P(AXES, None),
            P(None, AXES, None), P(), P(AXES, None), P(AXES, None), P(AXES, None, None, None),
        ),
        out_specs=(P(None, AXES, None), P(None, AXES, None), P(None, AXES, None)),
        check_vma=False,
    )
```

```python
import functools

import jax
import jax.numpy as jnp
from jax import lax
from jax.experimental import pallas as pl
from jax.experimental.pallas import tpu as pltpu
from jax.sharding import PartitionSpec as P

ATM_DIFFUSION = 0.1
OCEAN_DIFFUSION = 0.15
EXCHANGE_RATE = 0.3
FLUX_GAIN = 0.5
MESH = pl.DeviceIdType.MESH
AXES = ("comp", "tile")
F32 = jnp.float32
BF16 = jnp.bfloat16
G = 16
HBM = pl.BlockSpec(memory_space=pltpu.HBM)
LIMIT = 60 * 1024 * 1024


def iota(shape, dim):
    return lax.broadcasted_iota(jnp.int32, shape, dim)


def swap_matrix():
    a = iota((G * G, G * G), 0)
    b = iota((G * G, G * G), 1)
    return ((a // G == b % G) & (a % G == b // G)).astype(F32).astype(BF16)


def lateral_matrix(n):
    a = iota((n, n), 0)
    b = iota((n, n), 1)
    north = a == jnp.minimum(b + 1, n - 1)
    south = a == jnp.maximum(b - 1, 0)
    return (north.astype(F32) + south.astype(F32)).astype(BF16)


def dot(a, b):
    return jnp.dot(a, b, preferred_element_type=F32)


def dot_nt(a, b):
    return lax.dot_general(a, b, (((1,), (1,)), ((), ())), preferred_element_type=F32)


def dot_tn(a, b):
    return lax.dot_general(a, b, (((0,), (0,)), ((), ())), preferred_element_type=F32)


def edges_kernel(lo_ref, hi_ref, oc_ref, courant_ref, xe_ref, sst_ref, edge_ref, cr_ref):
    order = courant_ref.shape[1]
    diagonal = iota((order, order), 0) == iota((order, order), 1)
    cr_ref[...] = jnp.sum(jnp.where(diagonal, courant_ref[...], 0.0), axis=1, keepdims=True)
    width = oc_ref.shape[1]
    part = hi_ref.shape[1]
    sst_ref[...] = oc_ref[0].astype(BF16)
    edge_ref[0] = oc_ref[:, 0, :]
    edge_ref[1] = oc_ref[:, width - 1, :]
    swap = swap_matrix()
    picks = (swap[:G], swap[G * G - G :])
    cols = lo_ref.shape[2]
    for rb in range(lo_ref.shape[0] // G):
        for side, ref in enumerate((lo_ref, hi_ref)):
            block = ref[rb * G : (rb + 1) * G].reshape(G * part, cols)
            xe_ref[side, rb * G : (rb + 1) * G, :] = dot(picks[side], block).astype(BF16)


def edges(state, ocean, courant):
    rows, width, cols = state.shape
    orows, ow, oy = ocean.shape
    last = width // G - 1
    return pl.pallas_call(
        edges_kernel,
        grid=(1,),
        in_specs=[
            pl.BlockSpec((rows, G, cols), lambda g: (0, 0, 0)),
            pl.BlockSpec((rows, G, cols), lambda g: (0, last, 0)),
            pl.BlockSpec((orows, ow, oy), lambda g: (0, 0, 0)),
            pl.BlockSpec((1, rows), lambda g: (0, 0)),
        ],
        out_specs=[
            pl.BlockSpec((2, rows, cols), lambda g: (0, 0, 0)),
            pl.BlockSpec((ow, oy), lambda g: (0, 0)),
            pl.BlockSpec((2, orows, oy), lambda g: (0, 0, 0)),
            pl.BlockSpec((rows, 1), lambda g: (0, 0)),
        ],
        out_shape=[
            jax.ShapeDtypeStruct((2, rows, cols), BF16),
            jax.ShapeDtypeStruct((ow, oy), BF16),
            jax.ShapeDtypeStruct((2, orows, oy), F32),
            jax.ShapeDtypeStruct((rows, 1), F32),
        ],
        compiler_params=pltpu.CompilerParams(vmem_limit_bytes=LIMIT),
        name="edges",
    )(state, state, ocean, courant)


def place(index, tiles):
    return (index // tiles, index % tiles)


def my_index(tiles):
    return lax.axis_index("comp") * tiles + lax.axis_index("tile")


def greet_all(n, tiles, me):
    barrier = pltpu.get_barrier_semaphore()

    def signal(d, carry):
        pl.semaphore_signal(barrier, inc=1, device_id=place((me + d) % n, tiles), device_id_type=MESH)
        return carry

    lax.fori_loop(1, n, signal, 0)
    pl.semaphore_wait(barrier, n - 1)


def first_exchange_kernel(n, tiles, sst_ref, edge_ref, xe_ref, st_ref,
                          all_ref, halo_ref, ohalo, xs_ref, ssem, rsem, hs, hr, local):
    me = my_index(tiles)
    east = place((me + 1) % n, tiles)
    west = place((me + n - 1) % n, tiles)
    g = pl.program_id(0)

    def copy(d):
        return pltpu.make_async_remote_copy(
            src_ref=sst_ref, dst_ref=all_ref.at[me], send_sem=ssem.at[d], recv_sem=rsem.at[d],
            device_id=place((me + d) % n, tiles), device_id_type=MESH)

    moves = [
        (xe_ref.at[1], halo_ref.at[0], east),
        (xe_ref.at[0], halo_ref.at[1], west),
        (edge_ref.at[1], ohalo.at[0], east),
        (edge_ref.at[0], ohalo.at[1], west),
    ]
    copies = [
        pltpu.make_async_remote_copy(
            src_ref=s, dst_ref=d, send_sem=hs.at[i], recv_sem=hr.at[i], device_id=to, device_id_type=MESH)
        for i, (s, d, to) in enumerate(moves)
    ]
    own = pltpu.make_async_copy(sst_ref, all_ref.at[me], local)
    columns = st_ref.shape[2]

    @pl.when(g == 0)
    def _():
        greet_all(n, tiles, me)

        def start(d, carry):
            copy(d).start()
            return carry

        lax.fori_loop(1, n, start, 0)
        for c in copies:
            c.start()
        own.start()

    swap = swap_matrix()
    for rb in range(st_ref.shape[0] // G):
        block = st_ref[rb * G : (rb + 1) * G].reshape(G * G, columns)
        xs_ref[:, rb * G : (rb + 1) * G, :] = dot(swap, block).astype(BF16).reshape(G, G, columns)

    @pl.when(g == pl.num_programs(0) - 1)
    def _():
        for c in copies:
            c.wait()
        own.wait()

        def finish(d, carry):
            copy(d).wait()
            return carry

        lax.fori_loop(1, n, finish, 0)


def first_exchange(n, tiles, sst, edge, xe, state):
    rows, width, cols = state.shape
    dma = pltpu.SemaphoreType.DMA
    return pl.pallas_call(
        functools.partial(first_exchange_kernel, n, tiles),
        grid=(width // G,),
        in_specs=[HBM, HBM, HBM, pl.BlockSpec((rows, G, cols), lambda g: (0, g, 0))],
        out_specs=[HBM, HBM, HBM, pl.BlockSpec((G, rows, cols), lambda g: (g, 0, 0))],
        out_shape=[
            jax.ShapeDtypeStruct((n,) + sst.shape, BF16),
            jax.ShapeDtypeStruct((2, rows, cols), BF16),
            jax.ShapeDtypeStruct(edge.shape, F32),
            jax.ShapeDtypeStruct((width, rows, cols), BF16),
        ],
        scratch_shapes=[dma((n,)), dma((n,)), dma((4,)), dma((4,)), dma],
        compiler_params=pltpu.CompilerParams(collective_id=0, has_side_effects=True, vmem_limit_bytes=LIMIT),
        name="first_exchange",
    )(sst, edge, xe, state)


def one_hot(owner_ref, block_ref, k, count, per):
    target = owner_ref[k : k + 1, :] * per + block_ref[k : k + 1, :]
    return (iota((count, target.shape[1]), 0) == target).astype(F32).astype(BF16)


def slab_update(xs_ref, halo_ref, x, first, last, cr, lateral):
    width = xs_ref.shape[0]
    center = xs_ref[x]
    west = xs_ref[jnp.maximum(x - 1, 0)]
    east = xs_ref[jnp.minimum(x + 1, width - 1)]
    if first:
        west = jnp.where(x == 0, halo_ref[0], west)
    if last:
        east = jnp.where(x == width - 1, halo_ref[1], east)
    sides = dot(center, lateral) + east.astype(F32)
    return (
        (1.0 - 4.0 * ATM_DIFFUSION - cr) * center.astype(F32)
        + (cr + ATM_DIFFUSION) * west.astype(F32)
        + ATM_DIFFUSION * sides
    )


def force(updated, f_ref, heat, moist):
    rows = updated.shape[0]
    half = rows // 2
    f_ref[...] = updated.astype(BF16)
    last = iota((G, 1), 0) == G - 1
    for end, added in ((half, heat), (rows, moist)):
        part = updated[end - G : end]
        f_ref[end - G : end, :] = jnp.where(last, part + added, part).astype(BF16)


def step_one_kernel(n, tiles, xs_ref, halo_ref, all_ref, owner_ref, block_ref, w_ref, sea_ref, cr_ref, v_ref,
                    new_ref, temp_ref, heat_ref, moist_ref, r0_ref, r1_ref, halo2_ref, fetched, forced, ends, hs, hr):
    step = pl.program_id(0)
    steps = pl.num_programs(0)
    g = (step + steps - 1) % steps
    me = my_index(tiles)
    east = place((me + 1) % n, tiles)
    west = place((me + n - 1) % n, tiles)
    copies = [
        pltpu.make_async_remote_copy(
            src_ref=ends.at[i], dst_ref=halo2_ref.at[i], send_sem=hs.at[i], recv_sem=hr.at[i],
            device_id=to, device_id_type=MESH)
        for i, to in enumerate((east, west))
    ]

    @pl.when(step == 0)
    def _():
        barrier = pltpu.get_barrier_semaphore()
        for to in (east, west):
            pl.semaphore_signal(barrier, inc=1, device_id=to, device_id_type=MESH)
        pl.semaphore_wait(barrier, 2)

    for i in range(2):

        @pl.when(step == i + 1)
        def _():
            copies[i].start()

    xg = new_ref.shape[0]
    jg, kk, block, _ = w_ref.shape
    count = all_ref.shape[0] * all_ref.shape[1]

    @pl.when(step == 0)
    def _():
        table = all_ref[...].reshape(count, block)
        for k in range(kk):
            hot = one_hot(owner_ref, block_ref, k, count, all_ref.shape[1])
            fetched[k] = dot_tn(hot, table).astype(BF16)

    rows = xs_ref.shape[1]
    half = rows // 2
    lateral = lateral_matrix(xs_ref.shape[2])
    vertical = v_ref[...]
    cr = cr_ref[...]
    j0 = pl.multiple_of(g * jg, jg)
    sources = [fetched[k, pl.ds(j0, jg), :] for k in range(kk)]
    per = jg // xg
    for i in range(xg):
        temps = []
        for j in range(per * i, per * i + per):
            total = dot_nt(sources[0], w_ref[j, 0])
            for k in range(1, kk):
                total = total + dot_nt(sources[k], w_ref[j, k])
            temps.append(total[j : j + 1])
        temp = jnp.concatenate(temps, axis=1)
        updated = slab_update(xs_ref, halo_ref, g * xg + i, i == 0, i == xg - 1, cr, lateral)
        sea = EXCHANGE_RATE * sea_ref[i : i + 1, :].astype(F32)
        heat = sea * (temp - updated[half - 1 : half])
        moist = sea * (0.5 * temp - updated[rows - 1 : rows])
        slot = forced.at[i % 2]
        force(updated, slot, heat, moist)
        mixed = dot(vertical, slot[...]).astype(BF16)
        new_ref[i] = mixed
        temp_ref[i : i + 1, :] = temp
        heat_ref[i : i + 1, :] = heat
        moist_ref[i : i + 1, :] = moist
        r0_ref[i : i + 1, :] = mixed[half - G : half].astype(F32)[G - 1 : G]
        r1_ref[i : i + 1, :] = mixed[rows - G : rows].astype(F32)[G - 1 : G]

    @pl.when(step == 0)
    def _():
        ends[0] = new_ref[xg - 1]

    @pl.when(step == 1)
    def _():
        ends[1] = new_ref[0]

    @pl.when(step == steps - 1)
    def _():
        for c in copies:
            c.wait()


def whole(shape):
    return pl.BlockSpec(shape, lambda g: (0,) * len(shape))


def step_one(n, tiles, xs, halo, all_sst, owner, blocks, weight, sea, cr, vertical):
    width, rows, cols = xs.shape
    jb, kk, block, _ = weight.shape
    xg = 8
    steps = width // xg
    jg = jb // steps
    dma = pltpu.SemaphoreType.DMA

    def turn(g):
        return (g + steps - 1) % steps

    row = pl.BlockSpec((xg, cols), lambda g: (turn(g), 0))
    rowshape = jax.ShapeDtypeStruct((width, cols), F32)
    return pl.pallas_call(
        functools.partial(step_one_kernel, n, tiles),
        grid=(steps,),
        in_specs=[
            whole(xs.shape), whole(halo.shape), whole(all_sst.shape), whole(owner.shape), whole(blocks.shape),
            pl.BlockSpec((jg, kk, block, block), lambda g: (turn(g), 0, 0, 0)),
            row, whole(cr.shape), whole(vertical.shape),
        ],
        out_specs=[pl.BlockSpec((xg, rows, cols), lambda g: (turn(g), 0, 0))] + [row] * 5 + [HBM],
        out_shape=[jax.ShapeDtypeStruct(xs.shape, BF16)] + [rowshape] * 5 + [jax.ShapeDtypeStruct(halo.shape, BF16)],
        scratch_shapes=[
            pltpu.VMEM((kk, jb, block), BF16), pltpu.VMEM((2, rows, cols), BF16), pltpu.VMEM((2, rows, cols), BF16),
            dma((2,)), dma((2,)),
        ],
        compiler_params=pltpu.CompilerParams(collective_id=1, has_side_effects=True, vmem_limit_bytes=LIMIT),
        name="step_one",
    )(xs, halo, all_sst, owner, blocks, weight, sea, cr, vertical)


def push_kernel(r0_ref, r1_ref, halo_ref, cr_ref, sea_ref, temp_ref, heat_ref, moist_ref, owner_ref, block_ref, w_ref,
                heat2_ref, moist2_ref, acc_ref, mean, shares):
    g = pl.program_id(0)
    width, cols = r0_ref.shape
    jg, kk, block, _ = w_ref.shape
    rows = halo_ref.shape[1]
    per_owner = acc_ref.shape[1]

    @pl.when(g == 0)
    def _():
        lateral = lateral_matrix(cols)
        sea = EXCHANGE_RATE * sea_ref[...].astype(F32)
        temp = temp_ref[...]
        for v, (ref, end, gain, old, out) in enumerate((
            (r0_ref, rows // 2, 1.0, heat_ref, heat2_ref),
            (r1_ref, rows, 0.5, moist_ref, moist2_ref),
        )):
            center = ref[...]
            hw = halo_ref[0, end - G : end, :].astype(F32)[G - 1 : G]
            he = halo_ref[1, end - G : end, :].astype(F32)[G - 1 : G]
            west = jnp.concatenate([hw, center[:-1]], axis=0)
            east = jnp.concatenate([center[1:], he], axis=0)
            cr = cr_ref[end - 1 : end, :]
            updated = (
                (1.0 - 4.0 * ATM_DIFFUSION - cr) * center
                + (cr + ATM_DIFFUSION) * west
                + ATM_DIFFUSION * (dot(center.astype(BF16), lateral) + east)
            )
            flux = sea * (gain * temp - updated)
            out[...] = flux
            mean[v] = (0.5 * old[...] + 0.5 * flux).astype(BF16).astype(F32)

    xg = width * jg // owner_ref.shape[1]
    per = jg // xg
    x0 = pl.multiple_of(g * xg, xg)
    lefts = [
        jnp.concatenate([mean[v, pl.ds(x0, xg), h * block : (h + 1) * block] for v in range(2)], axis=0).astype(BF16)
        for h in range(per)
    ]
    j0 = pl.multiple_of(g * jg, jg)
    for k in range(kk):
        rows_of = []
        for j in range(jg):
            i = j // per
            share = dot(lefts[j % per], w_ref[j, k])
            rows_of.append(jnp.concatenate([share[i : i + 1], share[xg + i : xg + i + 1]], axis=1))
        shares[k, pl.ds(j0, jg), :] = jnp.concatenate(rows_of, axis=0)

    @pl.when(g == pl.num_programs(0) - 1)
    def _():
        count = acc_ref.shape[0] * per_owner
        total = jnp.zeros((count, 2 * block), F32)
        for k in range(kk):
            hot = one_hot(owner_ref, block_ref, k, count, per_owner)
            share = shares[k]
            high = share.astype(BF16)
            low = (share - high.astype(F32)).astype(BF16)
            total = total + dot(hot, high) + dot(hot, low)
        acc_ref[...] = total.astype(BF16).reshape(acc_ref.shape)


def push(n, per_owner, r0, r1, halo, cr, sea, temp, heat, moist, owner, blocks, weight):
    width, cols = r0.shape
    jb, kk, block, _ = weight.shape
    steps = width // 8
    jg = jb // steps
    return pl.pallas_call(
        push_kernel,
        grid=(steps,),
        in_specs=[whole(a.shape) for a in (r0, r1, halo, cr, sea, temp, heat, moist, owner, blocks)]
        + [pl.BlockSpec((jg, kk, block, block), lambda g: (g, 0, 0, 0))],
        out_specs=[whole(r0.shape), whole(r0.shape), whole((n, per_owner, 2 * block))],
        out_shape=[
            jax.ShapeDtypeStruct(r0.shape, F32),
            jax.ShapeDtypeStruct(r0.shape, F32),
            jax.ShapeDtypeStruct((n, per_owner, 2 * block), BF16),
        ],
        scratch_shapes=[pltpu.VMEM((2, width, cols), F32), pltpu.VMEM((kk, jb, 2 * block), F32)],
        compiler_params=pltpu.CompilerParams(vmem_limit_bytes=LIMIT),
        name="push",
    )(r0, r1, halo, cr, sea, temp, heat, moist, owner, blocks, weight)


def step_two_kernel(n, tiles, acc_ref, osea_ref, xs_ref, halo_ref, heat_ref, moist_ref, cr_ref, v_ref,
                    oc_ref, ohalo_ref, fin_ref, ov_ref, out_ref, flux_ref, ocean_ref, forced, land, ssem, rsem, local):
    me = my_index(tiles)
    g = pl.program_id(0)

    def copy(d):
        to = (me + d) % n
        return pltpu.make_async_remote_copy(
            src_ref=acc_ref.at[to], dst_ref=land.at[d], send_sem=ssem.at[d], recv_sem=rsem.at[d],
            device_id=place(to, tiles), device_id_type=MESH)

    own = pltpu.make_async_copy(acc_ref.at[me], land.at[0], local)

    @pl.when(g == 0)
    def _():
        greet_all(n, tiles, me)

        def start(d, carry):
            copy(d).start()
            return carry

        lax.fori_loop(1, n, start, 0)
        own.start()

    cols = xs_ref.shape[2]
    lateral = lateral_matrix(cols)
    vertical = v_ref[...]
    cr = cr_ref[...]
    for i in range(G):
        updated = slab_update(xs_ref, halo_ref, g * G + i, i == 0, i == G - 1, cr, lateral)
        slot = forced.at[i % 2]
        force(updated, slot, heat_ref[i : i + 1, :], moist_ref[i : i + 1, :])
        out_ref[i] = dot(vertical, slot[...]).astype(BF16)

    @pl.when(g == pl.num_programs(0) - 1)
    def _():
        ocean_columns(range(oc_ref.shape[1]), oc_ref, ohalo_ref, osea_ref, fin_ref, ov_ref, ocean_ref)
        own.wait()

        def finish(d, total):
            copy(d).wait()
            return total + land[d].astype(F32)

        total = lax.fori_loop(1, n, finish, land[0].astype(F32))
        sea = osea_ref[...].astype(F32)
        block = sea.shape[1]
        flux_ref[0] = total[:, :block] * sea
        flux_ref[1] = total[:, block:] * sea


def step_two(n, tiles, acc, osea, xs, halo, heat, moist, cr, vertical, ocean, ohalo, flux_in, overtical):
    width, rows, cols = xs.shape
    dma = pltpu.SemaphoreType.DMA
    row = pl.BlockSpec((G, cols), lambda g: (g, 0))
    return pl.pallas_call(
        functools.partial(step_two_kernel, n, tiles),
        grid=(width // G,),
        in_specs=[HBM, whole(osea.shape), whole(xs.shape), whole(halo.shape), row, row, whole(cr.shape),
                  whole(vertical.shape)] + [whole(a.shape) for a in (ocean, ohalo, flux_in, overtical)],
        out_specs=[pl.BlockSpec((G, rows, cols), lambda g: (g, 0, 0)), whole((2,) + osea.shape), whole(ocean.shape)],
        out_shape=[
            jax.ShapeDtypeStruct((width, rows, cols), BF16),
            jax.ShapeDtypeStruct((2,) + osea.shape, F32),
            jax.ShapeDtypeStruct(ocean.shape, F32),
        ],
        scratch_shapes=[
            pltpu.VMEM((2, rows, cols), BF16), pltpu.VMEM(acc.shape, BF16),
            dma((n,)), dma((n,)), dma,
        ],
        compiler_params=pltpu.CompilerParams(collective_id=2, has_side_effects=True, vmem_limit_bytes=LIMIT),
        name="step_two",
    )(acc, osea, xs, halo, heat, moist, cr, vertical, ocean, ohalo, flux_in, overtical)


def restore_kernel(new_ref, out_ref):
    cols = new_ref.shape[2]
    swap = swap_matrix()
    for rb in range(out_ref.shape[0] // G):
        block = new_ref[:, rb * G : (rb + 1) * G, :].reshape(G * G, cols)
        out_ref[rb * G : (rb + 1) * G] = dot(swap, block).astype(BF16).reshape(G, G, cols)


def restore(new):
    width, rows, cols = new.shape
    part = rows // 2
    return pl.pallas_call(
        restore_kernel,
        grid=(2, width // G),
        in_specs=[pl.BlockSpec((G, part, cols), lambda r, g: (g, r, 0))],
        out_specs=pl.BlockSpec((part, G, cols), lambda r, g: (r, g, 0)),
        out_shape=jax.ShapeDtypeStruct((rows, width, cols), BF16),
        compiler_params=pltpu.CompilerParams(vmem_limit_bytes=LIMIT),
        name="restore",
    )(new)


def ocean_columns(columns, oc_ref, halo_ref, sea_ref, flux_ref, v_ref, out_ref):
    rows, width, cols = oc_ref.shape
    half = rows // 2
    vertical = v_ref[...]
    vhigh = vertical.astype(BF16)
    vlow = (vertical - vhigh.astype(F32)).astype(BF16)
    lane = iota((1, cols), 1)
    row = iota((rows, 1), 0)
    for x in columns:
        center = oc_ref[:, x, :]
        west = halo_ref[0] if x == 0 else oc_ref[:, x - 1, :]
        east = halo_ref[1] if x == width - 1 else oc_ref[:, x + 1, :]
        north = jnp.where(lane == cols - 1, center, pltpu.roll(center, cols - 1, 1))
        south = jnp.where(lane == 0, center, pltpu.roll(center, 1, 1))
        tendency = east + west + (north + south) - 4.0 * center
        sea = sea_ref[x : x + 1, :].astype(F32)
        heat = FLUX_GAIN * sea * flux_ref[0, x : x + 1, :]
        fresh = FLUX_GAIN * sea * flux_ref[1, x : x + 1, :]
        updated = (center + OCEAN_DIFFUSION * tendency) * sea
        updated = updated + jnp.where(row == 0, heat, jnp.where(row == half, fresh, 0.0))
        high = updated.astype(BF16)
        low = (updated - high.astype(F32)).astype(BF16)
        mixed = dot(vhigh, high) + (dot(vhigh, low) + dot(vlow, high))
        out_ref[:, x, :] = mixed


def per_device(n, tiles, atm_state, atm_sea, zonal_courant, atm_vertical, ocean_state, ocean_sea, flux_in,
               ocean_vertical, remap_owner, remap_block, remap_weight):
    owner = remap_owner.T
    blocks = remap_block.T
    xe, sst, edge, cr = edges(atm_state, ocean_state, zonal_courant.reshape(1, -1))
    all_sst, halo, ohalo, xs = first_exchange(n, tiles, sst, edge, xe, atm_state)
    new, temp, heat, moist, r0, r1, halo2 = step_one(
        n, tiles, xs, halo, all_sst, owner, blocks, remap_weight, atm_sea, cr, atm_vertical)
    heat2, moist2, acc = push(
        n, sst.shape[0], r0, r1, halo2, cr, atm_sea, temp, heat, moist, owner, blocks, remap_weight)
    final, ocean_flux, ocean_next = step_two(
        n, tiles, acc, ocean_sea, new, halo2, heat2, moist2, cr, atm_vertical,
        ocean_state, ohalo, flux_in, ocean_vertical)
    return restore(final), ocean_next, ocean_flux


def solution(mesh):
    tiles = mesh.shape["tile"]
    n = mesh.shape["comp"] * tiles
    return jax.shard_map(
        functools.partial(per_device, n, tiles),
        mesh=mesh,
        in_specs=(
            P(None, AXES, None), P(AXES, None), P(), P(), P(None, AXES, None), P(AXES, None),
            P(None, AXES, None), P(), P(AXES, None), P(AXES, None), P(AXES, None, None, None),
        ),
        out_specs=(P(None, AXES, None), P(None, AXES, None), P(None, AXES, None)),
        check_vma=False,
    )
```

```python
import functools

import jax
import jax.numpy as jnp
from jax import lax
from jax.experimental import pallas as pl
from jax.experimental.pallas import tpu as pltpu
from jax.sharding import PartitionSpec as P

ATM_DIFFUSION = 0.1
OCEAN_DIFFUSION = 0.15
EXCHANGE_RATE = 0.3
FLUX_GAIN = 0.5
MESH = pl.DeviceIdType.MESH
AXES = ("comp", "tile")
F32 = jnp.float32
BF16 = jnp.bfloat16
G = 16
HBM = pl.BlockSpec(memory_space=pltpu.HBM)
LIMIT = 60 * 1024 * 1024


def iota(shape, dim):
    return lax.broadcasted_iota(jnp.int32, shape, dim)


def swap_matrix():
    a = iota((G * G, G * G), 0)
    b = iota((G * G, G * G), 1)
    return ((a // G == b % G) & (a % G == b // G)).astype(F32).astype(BF16)


def lateral_matrix(n):
    a = iota((n, n), 0)
    b = iota((n, n), 1)
    north = a == jnp.minimum(b + 1, n - 1)
    south = a == jnp.maximum(b - 1, 0)
    return (north.astype(F32) + south.astype(F32)).astype(BF16)


def dot(a, b):
    return jnp.dot(a, b, preferred_element_type=F32)


def dot_nt(a, b):
    return lax.dot_general(a, b, (((1,), (1,)), ((), ())), preferred_element_type=F32)


def dot_tn(a, b):
    return lax.dot_general(a, b, (((0,), (0,)), ((), ())), preferred_element_type=F32)


def edges_kernel(lo_ref, hi_ref, oc_ref, courant_ref, xe_ref, sst_ref, edge_ref, cr_ref):
    order = courant_ref.shape[1]
    diagonal = iota((order, order), 0) == iota((order, order), 1)
    cr_ref[...] = jnp.sum(jnp.where(diagonal, courant_ref[...], 0.0), axis=1, keepdims=True)
    width = oc_ref.shape[1]
    part = hi_ref.shape[1]
    sst_ref[...] = oc_ref[0].astype(BF16)
    edge_ref[0] = oc_ref[:, 0, :]
    edge_ref[1] = oc_ref[:, width - 1, :]
    swap = swap_matrix()
    picks = (swap[:G], swap[G * G - G :])
    cols = lo_ref.shape[2]
    for rb in range(lo_ref.shape[0] // G):
        for side, ref in enumerate((lo_ref, hi_ref)):
            block = ref[rb * G : (rb + 1) * G].reshape(G * part, cols)
            xe_ref[side, rb * G : (rb + 1) * G, :] = dot(picks[side], block).astype(BF16)


def edges(state, ocean, courant):
    rows, width, cols = state.shape
    orows, ow, oy = ocean.shape
    last = width // G - 1
    return pl.pallas_call(
        edges_kernel,
        grid=(1,),
        in_specs=[
            pl.BlockSpec((rows, G, cols), lambda g: (0, 0, 0)),
            pl.BlockSpec((rows, G, cols), lambda g: (0, last, 0)),
            pl.BlockSpec((orows, ow, oy), lambda g: (0, 0, 0)),
            pl.BlockSpec((1, rows), lambda g: (0, 0)),
        ],
        out_specs=[
            pl.BlockSpec((2, rows, cols), lambda g: (0, 0, 0)),
            pl.BlockSpec((ow, oy), lambda g: (0, 0)),
            pl.BlockSpec((2, orows, oy), lambda g: (0, 0, 0)),
            pl.BlockSpec((rows, 1), lambda g: (0, 0)),
        ],
        out_shape=[
            jax.ShapeDtypeStruct((2, rows, cols), BF16),
            jax.ShapeDtypeStruct((ow, oy), BF16),
            jax.ShapeDtypeStruct((2, orows, oy), F32),
            jax.ShapeDtypeStruct((rows, 1), F32),
        ],
        compiler_params=pltpu.CompilerParams(vmem_limit_bytes=LIMIT),
        name="edges",
    )(state, state, ocean, courant)


def place(index, tiles):
    return (index // tiles, index % tiles)


def my_index(tiles):
    return lax.axis_index("comp") * tiles + lax.axis_index("tile")


def greet_all(n, tiles, me):
    barrier = pltpu.get_barrier_semaphore()

    def signal(d, carry):
        pl.semaphore_signal(barrier, inc=1, device_id=place((me + d) % n, tiles), device_id_type=MESH)
        return carry

    lax.fori_loop(1, n, signal, 0)
    pl.semaphore_wait(barrier, n - 1)


def first_exchange_kernel(n, tiles, sst_ref, edge_ref, xe_ref, st_ref, oc_ref, sea_ref, flux_ref, v_ref,
                          all_ref, halo_ref, xs_ref, ocean_ref, ohalo, ssem, rsem, hs, hr, local):
    me = my_index(tiles)
    east = place((me + 1) % n, tiles)
    west = place((me + n - 1) % n, tiles)
    g = pl.program_id(0)

    def copy(d):
        return pltpu.make_async_remote_copy(
            src_ref=sst_ref, dst_ref=all_ref.at[me], send_sem=ssem.at[d], recv_sem=rsem.at[d],
            device_id=place((me + d) % n, tiles), device_id_type=MESH)

    moves = [
        (xe_ref.at[1], halo_ref.at[0], east),
        (xe_ref.at[0], halo_ref.at[1], west),
        (edge_ref.at[1], ohalo.at[0], east),
        (edge_ref.at[0], ohalo.at[1], west),
    ]
    copies = [
        pltpu.make_async_remote_copy(
            src_ref=s, dst_ref=d, send_sem=hs.at[i], recv_sem=hr.at[i], device_id=to, device_id_type=MESH)
        for i, (s, d, to) in enumerate(moves)
    ]
    own = pltpu.make_async_copy(sst_ref, all_ref.at[me], local)
    width = oc_ref.shape[1]
    columns = st_ref.shape[2]

    @pl.when(g == 0)
    def _():
        greet_all(n, tiles, me)

        def start(d, carry):
            copy(d).start()
            return carry

        for c in copies:
            c.start()
        lax.fori_loop(1, n, start, 0)
        own.start()

    swap = swap_matrix()
    for rb in range(st_ref.shape[0] // G):
        block = st_ref[rb * G : (rb + 1) * G].reshape(G * G, columns)
        xs_ref[:, rb * G : (rb + 1) * G, :] = dot(swap, block).astype(BF16).reshape(G, G, columns)

    @pl.when(g == 0)
    def _():
        ocean_columns(range(1, width - 1), oc_ref, ohalo, sea_ref, flux_ref, v_ref, ocean_ref)

    @pl.when(g == pl.num_programs(0) - 1)
    def _():
        for c in copies:
            c.wait()
        ocean_columns((0, width - 1), oc_ref, ohalo, sea_ref, flux_ref, v_ref, ocean_ref)
        own.wait()

        def finish(d, carry):
            copy(d).wait()
            return carry

        lax.fori_loop(1, n, finish, 0)


def first_exchange(n, tiles, sst, edge, xe, state, ocean, sea, flux, vertical):
    rows, width, cols = state.shape
    dma = pltpu.SemaphoreType.DMA
    return pl.pallas_call(
        functools.partial(first_exchange_kernel, n, tiles),
        grid=(width // G,),
        in_specs=[HBM, HBM, HBM, pl.BlockSpec((rows, G, cols), lambda g: (0, g, 0))]
        + [whole(a.shape) for a in (ocean, sea, flux, vertical)],
        out_specs=[HBM, HBM, pl.BlockSpec((G, rows, cols), lambda g: (g, 0, 0)), whole(ocean.shape)],
        out_shape=[
            jax.ShapeDtypeStruct((n,) + sst.shape, BF16),
            jax.ShapeDtypeStruct((2, rows, cols), BF16),
            jax.ShapeDtypeStruct((width, rows, cols), BF16),
            jax.ShapeDtypeStruct(ocean.shape, F32),
        ],
        scratch_shapes=[pltpu.VMEM(edge.shape, F32), dma((n,)), dma((n,)), dma((4,)), dma((4,)), dma],
        compiler_params=pltpu.CompilerParams(collective_id=0, has_side_effects=True, vmem_limit_bytes=LIMIT),
        name="first_exchange",
    )(sst, edge, xe, state, ocean, sea, flux, vertical)


def one_hot(owner_ref, block_ref, k, count, per):
    target = owner_ref[k : k + 1, :] * per + block_ref[k : k + 1, :]
    return (iota((count, target.shape[1]), 0) == target).astype(F32).astype(BF16)


def slab_update(xs_ref, halo_ref, x, first, last, cr, lateral):
    width = xs_ref.shape[0]
    center = xs_ref[x]
    west = xs_ref[jnp.maximum(x - 1, 0)]
    east = xs_ref[jnp.minimum(x + 1, width - 1)]
    if first:
        west = jnp.where(x == 0, halo_ref[0], west)
    if last:
        east = jnp.where(x == width - 1, halo_ref[1], east)
    sides = dot(center, lateral) + east.astype(F32)
    return (
        (1.0 - 4.0 * ATM_DIFFUSION - cr) * center.astype(F32)
        + (cr + ATM_DIFFUSION) * west.astype(F32)
        + ATM_DIFFUSION * sides
    )


def force(updated, f_ref, heat, moist):
    rows = updated.shape[0]
    half = rows // 2
    f_ref[...] = updated.astype(BF16)
    last = iota((G, 1), 0) == G - 1
    for end, added in ((half, heat), (rows, moist)):
        part = updated[end - G : end]
        f_ref[end - G : end, :] = jnp.where(last, part + added, part).astype(BF16)


def step_one_kernel(n, tiles, xs_ref, halo_ref, all_ref, owner_ref, block_ref, w_ref, sea_ref, cr_ref, v_ref,
                    new_ref, temp_ref, heat_ref, moist_ref, r0_ref, r1_ref, halo2_ref, fetched, forced, ends, hs, hr):
    step = pl.program_id(0)
    steps = pl.num_programs(0)
    g = (step + steps - 1) % steps
    me = my_index(tiles)
    east = place((me + 1) % n, tiles)
    west = place((me + n - 1) % n, tiles)
    copies = [
        pltpu.make_async_remote_copy(
            src_ref=ends.at[i], dst_ref=halo2_ref.at[i], send_sem=hs.at[i], recv_sem=hr.at[i],
            device_id=to, device_id_type=MESH)
        for i, to in enumerate((east, west))
    ]

    @pl.when(step == 0)
    def _():
        barrier = pltpu.get_barrier_semaphore()
        for to in (east, west):
            pl.semaphore_signal(barrier, inc=1, device_id=to, device_id_type=MESH)
        pl.semaphore_wait(barrier, 2)

    for i in range(2):

        @pl.when(step == i + 1)
        def _():
            copies[i].start()

    xg = new_ref.shape[0]
    jg, kk, block, _ = w_ref.shape
    count = all_ref.shape[0] * all_ref.shape[1]

    @pl.when(step == 0)
    def _():
        table = all_ref[...].reshape(count, block)
        for k in range(kk):
            hot = one_hot(owner_ref, block_ref, k, count, all_ref.shape[1])
            fetched[k] = dot_tn(hot, table).astype(BF16)

    rows = xs_ref.shape[1]
    half = rows // 2
    lateral = lateral_matrix(xs_ref.shape[2])
    vertical = v_ref[...]
    cr = cr_ref[...]
    j0 = pl.multiple_of(g * jg, jg)
    sources = [fetched[k, pl.ds(j0, jg), :] for k in range(kk)]
    per = jg // xg
    for i in range(xg):
        temps = []
        for j in range(per * i, per * i + per):
            total = dot_nt(sources[0], w_ref[j, 0])
            for k in range(1, kk):
                total = total + dot_nt(sources[k], w_ref[j, k])
            temps.append(total[j : j + 1])
        temp = jnp.concatenate(temps, axis=1)
        updated = slab_update(xs_ref, halo_ref, g * xg + i, i == 0, i == xg - 1, cr, lateral)
        sea = EXCHANGE_RATE * sea_ref[i : i + 1, :].astype(F32)
        heat = sea * (temp - updated[half - 1 : half])
        moist = sea * (0.5 * temp - updated[rows - 1 : rows])
        slot = forced.at[i % 2]
        force(updated, slot, heat, moist)
        mixed = dot(vertical, slot[...]).astype(BF16)
        new_ref[i] = mixed
        temp_ref[i : i + 1, :] = temp
        heat_ref[i : i + 1, :] = heat
        moist_ref[i : i + 1, :] = moist
        r0_ref[i : i + 1, :] = mixed[half - G : half].astype(F32)[G - 1 : G]
        r1_ref[i : i + 1, :] = mixed[rows - G : rows].astype(F32)[G - 1 : G]

    @pl.when(step == 0)
    def _():
        ends[0] = new_ref[xg - 1]

    @pl.when(step == 1)
    def _():
        ends[1] = new_ref[0]

    @pl.when(step == steps - 1)
    def _():
        for c in copies:
            c.wait()


def whole(shape):
    return pl.BlockSpec(shape, lambda g: (0,) * len(shape))


def step_one(n, tiles, xs, halo, all_sst, owner, blocks, weight, sea, cr, vertical):
    width, rows, cols = xs.shape
    jb, kk, block, _ = weight.shape
    xg = 8
    steps = width // xg
    jg = jb // steps
    dma = pltpu.SemaphoreType.DMA

    def turn(g):
        return (g + steps - 1) % steps

    row = pl.BlockSpec((xg, cols), lambda g: (turn(g), 0))
    rowshape = jax.ShapeDtypeStruct((width, cols), F32)
    return pl.pallas_call(
        functools.partial(step_one_kernel, n, tiles),
        grid=(steps,),
        in_specs=[
            whole(xs.shape), whole(halo.shape), whole(all_sst.shape), whole(owner.shape), whole(blocks.shape),
            pl.BlockSpec((jg, kk, block, block), lambda g: (turn(g), 0, 0, 0)),
            row, whole(cr.shape), whole(vertical.shape),
        ],
        out_specs=[pl.BlockSpec((xg, rows, cols), lambda g: (turn(g), 0, 0))] + [row] * 5 + [HBM],
        out_shape=[jax.ShapeDtypeStruct(xs.shape, BF16)] + [rowshape] * 5 + [jax.ShapeDtypeStruct(halo.shape, BF16)],
        scratch_shapes=[
            pltpu.VMEM((kk, jb, block), BF16), pltpu.VMEM((2, rows, cols), BF16), pltpu.VMEM((2, rows, cols), BF16),
            dma((2,)), dma((2,)),
        ],
        compiler_params=pltpu.CompilerParams(collective_id=1, has_side_effects=True, vmem_limit_bytes=LIMIT),
        name="step_one",
    )(xs, halo, all_sst, owner, blocks, weight, sea, cr, vertical)


def push_kernel(r0_ref, r1_ref, halo_ref, cr_ref, sea_ref, temp_ref, heat_ref, moist_ref, owner_ref, block_ref, w_ref,
                heat2_ref, moist2_ref, acc_ref, mean, shares):
    g = pl.program_id(0)
    width, cols = r0_ref.shape
    jg, kk, block, _ = w_ref.shape
    rows = halo_ref.shape[1]
    per_owner = acc_ref.shape[1]

    @pl.when(g == 0)
    def _():
        lateral = lateral_matrix(cols)
        sea = EXCHANGE_RATE * sea_ref[...].astype(F32)
        temp = temp_ref[...]
        for v, (ref, end, gain, old, out) in enumerate((
            (r0_ref, rows // 2, 1.0, heat_ref, heat2_ref),
            (r1_ref, rows, 0.5, moist_ref, moist2_ref),
        )):
            center = ref[...]
            hw = halo_ref[0, end - G : end, :].astype(F32)[G - 1 : G]
            he = halo_ref[1, end - G : end, :].astype(F32)[G - 1 : G]
            west = jnp.concatenate([hw, center[:-1]], axis=0)
            east = jnp.concatenate([center[1:], he], axis=0)
            cr = cr_ref[end - 1 : end, :]
            updated = (
                (1.0 - 4.0 * ATM_DIFFUSION - cr) * center
                + (cr + ATM_DIFFUSION) * west
                + ATM_DIFFUSION * (dot(center.astype(BF16), lateral) + east)
            )
            flux = sea * (gain * temp - updated)
            out[...] = flux
            mean[v] = (0.5 * old[...] + 0.5 * flux).astype(BF16).astype(F32)

    xg = width * jg // owner_ref.shape[1]
    per = jg // xg
    x0 = pl.multiple_of(g * xg, xg)
    lefts = [
        jnp.concatenate([mean[v, pl.ds(x0, xg), h * block : (h + 1) * block] for v in range(2)], axis=0).astype(BF16)
        for h in range(per)
    ]
    j0 = pl.multiple_of(g * jg, jg)
    for k in range(kk):
        rows_of = []
        for j in range(jg):
            i = j // per
            share = dot(lefts[j % per], w_ref[j, k])
            rows_of.append(jnp.concatenate([share[i : i + 1], share[xg + i : xg + i + 1]], axis=1))
        shares[k, pl.ds(j0, jg), :] = jnp.concatenate(rows_of, axis=0)

    @pl.when(g == pl.num_programs(0) - 1)
    def _():
        count = acc_ref.shape[0] * per_owner
        total = jnp.zeros((count, 2 * block), F32)
        for k in range(kk):
            hot = one_hot(owner_ref, block_ref, k, count, per_owner)
            share = shares[k]
            high = share.astype(BF16)
            low = (share - high.astype(F32)).astype(BF16)
            total = total + dot(hot, high) + dot(hot, low)
        acc_ref[...] = total.astype(BF16).reshape(acc_ref.shape)


def push(n, per_owner, r0, r1, halo, cr, sea, temp, heat, moist, owner, blocks, weight):
    width, cols = r0.shape
    jb, kk, block, _ = weight.shape
    steps = width // 8
    jg = jb // steps
    return pl.pallas_call(
        push_kernel,
        grid=(steps,),
        in_specs=[whole(a.shape) for a in (r0, r1, halo, cr, sea, temp, heat, moist, owner, blocks)]
        + [pl.BlockSpec((jg, kk, block, block), lambda g: (g, 0, 0, 0))],
        out_specs=[whole(r0.shape), whole(r0.shape), whole((n, per_owner, 2 * block))],
        out_shape=[
            jax.ShapeDtypeStruct(r0.shape, F32),
            jax.ShapeDtypeStruct(r0.shape, F32),
            jax.ShapeDtypeStruct((n, per_owner, 2 * block), BF16),
        ],
        scratch_shapes=[pltpu.VMEM((2, width, cols), F32), pltpu.VMEM((kk, jb, 2 * block), F32)],
        compiler_params=pltpu.CompilerParams(vmem_limit_bytes=LIMIT),
        name="push",
    )(r0, r1, halo, cr, sea, temp, heat, moist, owner, blocks, weight)


def step_two_kernel(n, tiles, acc_ref, osea_ref, xs_ref, halo_ref, heat_ref, moist_ref, cr_ref, v_ref,
                    out_ref, flux_ref, forced, land, ssem, rsem, local):
    me = my_index(tiles)
    g = pl.program_id(0)

    def copy(d):
        to = (me + d) % n
        return pltpu.make_async_remote_copy(
            src_ref=acc_ref.at[to], dst_ref=land.at[d], send_sem=ssem.at[d], recv_sem=rsem.at[d],
            device_id=place(to, tiles), device_id_type=MESH)

    own = pltpu.make_async_copy(acc_ref.at[me], land.at[0], local)

    @pl.when(g == 0)
    def _():
        greet_all(n, tiles, me)

        def start(d, carry):
            copy(d).start()
            return carry

        lax.fori_loop(1, n, start, 0)
        own.start()

    cols = xs_ref.shape[2]
    lateral = lateral_matrix(cols)
    vertical = v_ref[...]
    cr = cr_ref[...]
    for i in range(G):
        updated = slab_update(xs_ref, halo_ref, g * G + i, i == 0, i == G - 1, cr, lateral)
        slot = forced.at[i % 2]
        force(updated, slot, heat_ref[i : i + 1, :], moist_ref[i : i + 1, :])
        out_ref[i] = dot(vertical, slot[...]).astype(BF16)

    @pl.when(g == pl.num_programs(0) - 1)
    def _():
        own.wait()

        def finish(d, total):
            copy(d).wait()
            return total + land[d].astype(F32)

        total = lax.fori_loop(1, n, finish, land[0].astype(F32))
        sea = osea_ref[...].astype(F32)
        block = sea.shape[1]
        flux_ref[0] = total[:, :block] * sea
        flux_ref[1] = total[:, block:] * sea


def step_two(n, tiles, acc, osea, xs, halo, heat, moist, cr, vertical):
    width, rows, cols = xs.shape
    dma = pltpu.SemaphoreType.DMA
    row = pl.BlockSpec((G, cols), lambda g: (g, 0))
    return pl.pallas_call(
        functools.partial(step_two_kernel, n, tiles),
        grid=(width // G,),
        in_specs=[HBM, whole(osea.shape), whole(xs.shape), whole(halo.shape), row, row, whole(cr.shape),
                  whole(vertical.shape)],
        out_specs=[pl.BlockSpec((G, rows, cols), lambda g: (g, 0, 0)), whole((2,) + osea.shape)],
        out_shape=[
            jax.ShapeDtypeStruct((width, rows, cols), BF16),
            jax.ShapeDtypeStruct((2,) + osea.shape, F32),
        ],
        scratch_shapes=[
            pltpu.VMEM((2, rows, cols), BF16), pltpu.VMEM(acc.shape, BF16),
            dma((n,)), dma((n,)), dma,
        ],
        compiler_params=pltpu.CompilerParams(collective_id=2, has_side_effects=True, vmem_limit_bytes=LIMIT),
        name="step_two",
    )(acc, osea, xs, halo, heat, moist, cr, vertical)


def restore_kernel(new_ref, out_ref):
    cols = new_ref.shape[2]
    swap = swap_matrix()
    for rb in range(out_ref.shape[0] // G):
        block = new_ref[:, rb * G : (rb + 1) * G, :].reshape(G * G, cols)
        out_ref[rb * G : (rb + 1) * G] = dot(swap, block).astype(BF16).reshape(G, G, cols)


def restore(new):
    width, rows, cols = new.shape
    part = rows // 2
    return pl.pallas_call(
        restore_kernel,
        grid=(2, width // G),
        in_specs=[pl.BlockSpec((G, part, cols), lambda r, g: (g, r, 0))],
        out_specs=pl.BlockSpec((part, G, cols), lambda r, g: (r, g, 0)),
        out_shape=jax.ShapeDtypeStruct((rows, width, cols), BF16),
        compiler_params=pltpu.CompilerParams(vmem_limit_bytes=LIMIT),
        name="restore",
    )(new)


def ocean_columns(columns, oc_ref, halo_ref, sea_ref, flux_ref, v_ref, out_ref):
    rows, width, cols = oc_ref.shape
    half = rows // 2
    vertical = v_ref[...]
    vhigh = vertical.astype(BF16)
    vlow = (vertical - vhigh.astype(F32)).astype(BF16)
    lane = iota((1, cols), 1)
    row = iota((rows, 1), 0)
    for x in columns:
        center = oc_ref[:, x, :]
        west = halo_ref[0] if x == 0 else oc_ref[:, x - 1, :]
        east = halo_ref[1] if x == width - 1 else oc_ref[:, x + 1, :]
        north = jnp.where(lane == cols - 1, center, pltpu.roll(center, cols - 1, 1))
        south = jnp.where(lane == 0, center, pltpu.roll(center, 1, 1))
        tendency = east + west + (north + south) - 4.0 * center
        sea = sea_ref[x : x + 1, :].astype(F32)
        heat = FLUX_GAIN * sea * flux_ref[0, x : x + 1, :]
        fresh = FLUX_GAIN * sea * flux_ref[1, x : x + 1, :]
        updated = (center + OCEAN_DIFFUSION * tendency) * sea
        updated = updated + jnp.where(row == 0, heat, jnp.where(row == half, fresh, 0.0))
        high = updated.astype(BF16)
        low = (updated - high.astype(F32)).astype(BF16)
        mixed = dot(vhigh, high) + (dot(vhigh, low) + dot(vlow, high))
        out_ref[:, x, :] = mixed


def per_device(n, tiles, atm_state, atm_sea, zonal_courant, atm_vertical, ocean_state, ocean_sea, flux_in,
               ocean_vertical, remap_owner, remap_block, remap_weight):
    owner = remap_owner.T
    blocks = remap_block.T
    xe, sst, edge, cr = edges(atm_state, ocean_state, zonal_courant.reshape(1, -1))
    all_sst, halo, xs, ocean_next = first_exchange(
        n, tiles, sst, edge, xe, atm_state, ocean_state, ocean_sea, flux_in, ocean_vertical)
    new, temp, heat, moist, r0, r1, halo2 = step_one(
        n, tiles, xs, halo, all_sst, owner, blocks, remap_weight, atm_sea, cr, atm_vertical)
    heat2, moist2, acc = push(
        n, sst.shape[0], r0, r1, halo2, cr, atm_sea, temp, heat, moist, owner, blocks, remap_weight)
    final, ocean_flux = step_two(n, tiles, acc, ocean_sea, new, halo2, heat2, moist2, cr, atm_vertical)
    return restore(final), ocean_next, ocean_flux


def solution(mesh):
    tiles = mesh.shape["tile"]
    n = mesh.shape["comp"] * tiles
    return jax.shard_map(
        functools.partial(per_device, n, tiles),
        mesh=mesh,
        in_specs=(
            P(None, AXES, None), P(AXES, None), P(), P(), P(None, AXES, None), P(AXES, None),
            P(None, AXES, None), P(), P(AXES, None), P(AXES, None), P(AXES, None, None, None),
        ),
        out_specs=(P(None, AXES, None), P(None, AXES, None), P(None, AXES, None)),
        check_vma=False,
    )
```
